512 devices in a mesh: tm: 64 (over y, z_lo, core), sta: 8 (over x, z_hi).
Axes of the slice: x: 4, y: 8, z: 8 (z_hi: 2, z_lo: 4; z = z_hi * 4 + z_lo), core: 2. Of those that a mesh axis runs over, the one named last changes fastest.
Arguments:
- data: bfloat16 [64, 3, 24576], P('sta', None, 'tm'), as said below
- bank: bfloat16 [64, 8, 64, 3, 150], P('tm', None, 'sta'), may hold values from -6 to 6
- owners: int32 [2], replicated, may hold values from 0 to 63
- moveouts: int32 [2, 8, 64], P(None, None, 'sta'), may hold values from 0 to 64, as said below
Outputs:
- stack: float32 [2, 8, 24576], P(None, 'sta', 'tm')
The draws below stay inside these ranges and needn't reach their ends.
Inputs may be any that keep to these rules, and one draw needn't show every extreme that they name: `data`: three-component records with amplitudes that vary from station to station and along time. `moveouts`: delays are relative to the earliest arrival: for each template some station has 0 and some other station has 64.
All inputs are finite; a program needn't handle non-finite values.
Results may differ from the reference program's by a relative error of at most 0.0003.
Values may be sent and summed in bfloat16 or wider, within the bound.
No kernel may reach another device: no remote copies, remote signals or barrier semaphores. Data moves between devices by JAX's collectives and lax.ppermute only.
A program may use at most 64 MiB of HBM per device.

```python
import math
import jax
import jax.numpy as jnp
from jax import lax

STA = 64
NTPL = 8
NB = 2
L = 150
MAXM = 64
NTIME = 24576
BANKS = 64
N_TM = 64


def draw_data(key, part):
    keys = jax.random.split(key, 2)
    shape = (STA, 3, NTIME)
    noise = jax.random.normal(keys[0], shape, jnp.float32)
    levels = jax.random.uniform(keys[1], (STA, 3, NTIME // 8), jnp.float32, 0.0, math.log(10.0))
    envelope = jnp.repeat(jnp.exp(levels), 8, axis=2)
    return (noise * envelope).astype(jnp.bfloat16)


def draw_moveouts(key, part):
    keys = jax.random.split(key, 3)
    delays = jax.random.randint(keys[0], (NB, NTPL, STA), 0, MAXM + 1)
    earliest = jax.random.randint(keys[1], (NB, NTPL, 1), 0, STA)
    stride = jax.random.randint(keys[2], (NB, NTPL, 1), 1, STA)
    farthest = (earliest + stride) % STA
    column = jnp.arange(STA, dtype=jnp.int32)[None, None, :]
    delays = jnp.where(column == earliest, 0, delays)
    delays = jnp.where(column == farthest, MAXM, delays)
    return delays.astype(jnp.int32)


def shard_levels(key, shape, pieces, smallest, high):
    gain = 1.0
    for position, shards_of in pieces:
        heights = jax.random.uniform(jax.random.fold_in(jax.random.fold_in(key, 6), position), (shards_of,), jnp.float32, smallest / len(pieces), high / len(pieces))
        gain = gain * jnp.repeat(jnp.exp(heights), shape[position] // shards_of).reshape((-1,) + (1,) * (len(shape) - 1 - position))
    return gain


def normal_values(rng, shape, width, limit, shards=(), kind=jnp.bfloat16):
    values = jax.random.normal(rng, shape, jnp.float32) * width
    if len(shards) > 0:
        values = shard_levels(rng, shape, shards, -0.22, 0.18) * values
    return jnp.clip(values, min=-limit, max=limit).astype(kind)


def setup_inputs(seed: int = 0) -> dict:
    key_list = jax.random.split(jax.random.key(seed), 5)
    return {
        "data": draw_data(jax.random.fold_in(key_list[4], 71), 0),
        "bank": normal_values(key_list[1], (BANKS, NTPL, STA, 3, L), 1.0, 6.0, ((0, 64), (2, 8))),
        "owners": jax.random.randint(key_list[2], (NB,), 0, N_TM).astype(jnp.int32),
        "moveouts": draw_moveouts(jax.random.fold_in(key_list[4], 71), 0),
    }


eps = 1e-06

def reference(data, bank, owners, moveouts):
    batches = jnp.take(bank, owners, axis=0)
    padded = jnp.pad(data, ((0, 0), (0, 0), (0, L - 1 + MAXM)))
    kernels = jnp.transpose(batches, (2, 0, 1, 3, 4)).reshape(STA, NB * NTPL, 3, L)
    delays = jnp.transpose(moveouts, (2, 0, 1)).reshape(STA, NB * NTPL)
    offsets = jnp.arange(NTIME, dtype=jnp.int32)

    def station_step(running, station_items):
        record, kernel, lag_row = station_items
        products = lax.conv_general_dilated(record[None], kernel, (1,), 'VALID', dimension_numbers=('NCH', 'OIH', 'NCH'), preferred_element_type=jnp.float32)[0]
        squares = lax.optimization_barrier(jnp.sum(jnp.square(record.astype(jnp.float32)), axis=0))
        energy = lax.reduce_window(squares, jnp.array(0.0, squares.dtype), lax.add, (L,), (1,), 'VALID') / (3 * L)
        tmpl_power = lax.optimization_barrier(jnp.sum(jnp.square(kernel.astype(jnp.float32)), axis=(1, 2))) / (3 * L)
        scores = products / (3 * L * jnp.sqrt(tmpl_power + eps)[:, None] * jnp.sqrt(energy + eps)[None, :])
        shifted = jnp.take_along_axis(scores, offsets[None, :] + lag_row.astype(jnp.int32)[:, None], axis=1)
        return (running + shifted, None)
    running, unused = lax.scan(station_step, jnp.zeros((NB * NTPL, NTIME), jnp.float32), (padded, kernels, delays))
    return running.reshape(NB, NTPL, NTIME)
```

```python
import jax
import jax.numpy as jnp
from jax import lax
from jax.experimental import pallas as pl
from jax.experimental.pallas import tpu as pltpu
from jax.sharding import PartitionSpec as P


MAXM = 64
STEP = 40
LANES = 128
WIN = 640

eps = 1e-06

VMEM = pl.BlockSpec(memory_space=pltpu.VMEM)
HBM = pl.BlockSpec(memory_space=pltpu.HBM)
LIMIT = pltpu.CompilerParams(vmem_limit_bytes=16 * 1024 * 1024)


def passed_along(block, axis, distance):
    devices = range(lax.axis_size(axis))
    route = [(i - distance, i) for i in devices if i - distance in devices]
    return lax.ppermute(block, axis, route)


def roll_left(value, amount):
    return pltpu.roll(value, value.shape[1] - amount, 1)


def pack_kernel(bank_hbm, data_hbm, owners_hbm, lags_hbm, out_ref, data_ref, owners_ref, lags_ref, bank_ref, given_ref, sems):
    moves = [
        pltpu.make_async_copy(bank_hbm, bank_ref, sems.at[0]),
        pltpu.make_async_copy(data_hbm, data_ref, sems.at[1]),
        pltpu.make_async_copy(owners_hbm, given_ref, sems.at[2]),
        pltpu.make_async_copy(lags_hbm, lags_ref, sems.at[3]),
    ]
    for move in moves:
        move.start()
    tmpl_count, comp_count, local_sta, span_len = bank_ref.shape
    groups = -(-span_len // STEP)
    rows = tmpl_count * local_sta
    lag = lax.broadcasted_iota(jnp.int32, (span_len, 1), 0)
    target = (lag // STEP) * LANES + lag % STEP
    lane = lax.broadcasted_iota(jnp.int32, (span_len, groups * LANES), 1)
    places = [
        jnp.where(lane == target + comp * STEP, 1.0, 0.0).astype(jnp.bfloat16) for comp in range(comp_count)
    ]
    to_row = lax.broadcasted_iota(jnp.int32, (rows * groups, 1), 0)
    source = ((to_row // groups) % tmpl_count) * local_sta + to_row // (groups * tmpl_count)
    from_row = lax.broadcasted_iota(jnp.int32, (rows * groups, rows), 1)
    reorders = [
        jnp.where(from_row == jnp.where(to_row % groups == group, source, -1), 1.0, 0.0).astype(jnp.bfloat16)
        for group in range(groups)
    ]
    moves[0].wait()
    packed = jnp.zeros((rows, groups * LANES), jnp.float32)
    for comp in range(comp_count):
        taps = bank_ref[:, comp].astype(jnp.float32).reshape(rows, span_len).astype(jnp.bfloat16)
        packed += jnp.dot(taps, places[comp], preferred_element_type=jnp.float32)
    packed = packed.astype(jnp.bfloat16)
    ordered = jnp.zeros((rows * groups, LANES), jnp.float32)
    for group in range(groups):
        piece = packed[:, group * LANES : (group + 1) * LANES]
        ordered += jnp.dot(reorders[group], piece, preferred_element_type=jnp.float32)
    out_ref[...] = ordered.astype(jnp.bfloat16)
    moves[2].wait()
    for b in range(owners_ref.shape[0]):
        owners_ref[b] = jnp.broadcast_to(given_ref[:, b : b + 1], owners_ref.shape[1:])
    moves[1].wait()
    moves[3].wait()


def pack(bank, data, owners, lags):
    tmpl_count, _, local_sta, span_len = bank.shape
    rows = local_sta * tmpl_count * -(-span_len // STEP)
    return pl.pallas_call(
        pack_kernel,
        out_shape=(
            jax.ShapeDtypeStruct((rows, LANES), jnp.bfloat16),
            jax.ShapeDtypeStruct(data.shape, data.dtype),
            jax.ShapeDtypeStruct((owners.shape[1], 8, LANES), jnp.int32),
            jax.ShapeDtypeStruct(lags.shape, lags.dtype),
        ),
        in_specs=[HBM] * 4,
        out_specs=(VMEM,) * 4,
        scratch_shapes=[
            pltpu.VMEM(bank.shape, bank.dtype),
            pltpu.VMEM(owners.shape, owners.dtype),
            pltpu.SemaphoreType.DMA((4,)),
        ],
        compiler_params=LIMIT,
        name="pack",
        cost_estimate=pl.CostEstimate(flops=40_000_000, bytes_accessed=200_000, transcendentals=0),
    )(*(pltpu.with_memory_space_constraint(x, pltpu.HBM) for x in (bank, data, owners, lags)))


def pick_kernel(owners_ref, seen_ref, out_ref):
    seen = seen_ref[...].astype(jnp.float32)
    _, groups, _ = seen.shape
    block = lax.broadcasted_iota(jnp.int32, seen.shape, 0)
    rows = []
    for b in range(owners_ref.shape[0]):
        chosen = block == owners_ref[b, :groups, :][None]
        rows.append(jnp.sum(jnp.where(chosen, seen, 0.0), axis=0))
    chunk = jnp.concatenate(rows, axis=0).astype(out_ref.dtype)
    out_ref[...] = jnp.broadcast_to(chunk[None], out_ref.shape)


def pick(owners, seen):
    blocks, groups, lanes = seen.shape
    return pl.pallas_call(
        pick_kernel,
        out_shape=jax.ShapeDtypeStruct((blocks, owners.shape[0] * groups, lanes), seen.dtype),
        in_specs=[VMEM, VMEM],
        out_specs=VMEM,
        compiler_params=LIMIT,
        name="pick",
        cost_estimate=pl.CostEstimate(flops=100_000, bytes_accessed=200_000, transcendentals=0),
    )(owners, seen)


def records_kernel(span_len, data_ref, edge_ref, hankel_ref, scale_ref):
    comp_count, local_sta, stretch_len = data_ref.shape
    row = lax.broadcasted_iota(jnp.int32, (8, WIN), 0)
    squares = jnp.zeros((local_sta, WIN), jnp.float32)
    windows = []
    for comp in range(comp_count):
        edge = edge_ref[comp, :, : WIN - stretch_len]
        record = jnp.concatenate([data_ref[comp].astype(jnp.float32), edge.astype(jnp.float32)], axis=1)
        squares += record * record
        windows.append(record)
    for sta in range(local_sta):
        parts = []
        for comp in range(comp_count):
            base = jnp.broadcast_to(windows[comp][sta : sta + 1], (8, WIN))
            for bit in (1, 2, 4):
                base = jnp.where((row & bit) != 0, roll_left(base, bit), base)
            parts += [base if lag == 0 else roll_left(base, lag) for lag in range(0, STEP, 8)]
        while len(parts) * 8 < LANES:
            parts.append(jnp.zeros((8, WIN), jnp.float32))
        for at in range(0, len(parts), 2):
            pair = jnp.concatenate(parts[at : at + 2], axis=0)
            hankel_ref[sta, at * 8 : at * 8 + 16, :] = pair.astype(jnp.bfloat16)
    run, total, at, width = squares, None, 0, 1
    while width <= span_len:
        if span_len & width:
            piece = run if at == 0 else roll_left(run, at)
            total = piece if total is None else total + piece
            at += width
        if 2 * width <= span_len:
            run = run + roll_left(run, width)
        width *= 2
    scale_ref[...] = 1.0 / jnp.sqrt(total / (comp_count * span_len) + eps)


def records(data, edge, span_len):
    _, local_sta, _ = data.shape
    return pl.pallas_call(
        lambda *refs: records_kernel(span_len, *refs),
        out_shape=(
            jax.ShapeDtypeStruct((local_sta, LANES, WIN), jnp.bfloat16),
            jax.ShapeDtypeStruct((local_sta, WIN), jnp.float32),
        ),
        in_specs=[VMEM, VMEM],
        out_specs=(VMEM, VMEM),
        compiler_params=LIMIT,
        name="records",
        cost_estimate=pl.CostEstimate(flops=8_000_000, bytes_accessed=4_000_000, transcendentals=4096),
    )(data, edge)


def stack_kernel(taps_count, tmpl_ref, hankel_ref, scale_ref, lag_ref, out_ref, wide_ref):
    tmpl_count, batch_count, stretch_len = out_ref.shape
    local_sta = hankel_ref.shape[0]
    groups = tmpl_ref.shape[1] // batch_count
    inner = batch_count * groups
    wide_ref[...] = tmpl_ref[...].astype(jnp.float32).reshape(wide_ref.shape)
    total = None
    for sta in range(local_sta):
        taps = []
        for group in range(groups):
            for batch in range(batch_count):
                start = sta * tmpl_count * inner + batch * groups + group
                taps.append(wide_ref[pl.ds(start, tmpl_count, stride=inner), :])
        left = jnp.concatenate(taps, axis=0)
        rows = batch_count * tmpl_count
        power = sum(left[g * rows : (g + 1) * rows] * left[g * rows : (g + 1) * rows] for g in range(groups))
        power = jnp.sum(power, axis=1, keepdims=True) / taps_count
        prods = jnp.dot(left.astype(jnp.bfloat16), hankel_ref[sta], preferred_element_type=jnp.float32)
        prod = prods[(groups - 1) * rows :]
        for group in range(groups - 2, -1, -1):
            prod = roll_left(prod, STEP) + prods[group * rows : (group + 1) * rows]
        scores = prod * (1.0 / (taps_count * jnp.sqrt(power + eps))) * scale_ref[sta : sta + 1, :]
        scores = scores[:, : stretch_len + 128]
        lags = lag_ref[:, sta : sta + 1]
        bit = 1
        while bit <= MAXM:
            scores = jnp.where((lags & bit) != 0, roll_left(scores, bit), scores)
            bit *= 2
        total = scores if total is None else total + scores
    for batch in range(batch_count):
        out_ref[:, batch, :] = total[batch * tmpl_count : (batch + 1) * tmpl_count, :stretch_len]


def stack(tmpl, hankel, scale, lags, taps_count, out_shape):
    return pl.pallas_call(
        lambda *refs: stack_kernel(taps_count, *refs),
        out_shape=jax.ShapeDtypeStruct(out_shape, jnp.float32),
        in_specs=[VMEM] * 4,
        out_specs=VMEM,
        scratch_shapes=[pltpu.VMEM((tmpl.shape[0] * tmpl.shape[1], LANES), jnp.float32)],
        compiler_params=LIMIT,
        name="stack",
        cost_estimate=pl.CostEstimate(flops=60_000_000, bytes_accessed=4_000_000, transcendentals=4096),
    )(tmpl, hankel, scale, lags)


def shards(data, bank, owners, moveouts):
    local_sta, comp_count, stretch_len = data.shape
    span_len = bank.shape[-1]
    tmpl_count = bank.shape[1]
    batch_count = owners.shape[0]
    blocks = lax.axis_size("tm")
    source = jnp.transpose(data, (1, 0, 2))
    lags = moveouts.reshape(batch_count * tmpl_count, local_sta)
    slot, series, owned, lags = pack(jnp.transpose(bank[0], (0, 2, 1, 3)), source, owners[None], lags)
    seen = lax.all_to_all(slot.reshape(blocks, -1, LANES), "tm", 0, 0, tiled=True)
    edge = passed_along(source, "tm", -1)
    chosen = pick(owned, seen)
    tmpl = lax.all_to_all(chosen, "tm", 0, 0, tiled=True)
    hankel, scale = records(series, edge, span_len)
    partial_sum = stack(
        tmpl, hankel, scale, lags, comp_count * span_len, (tmpl_count, batch_count, stretch_len)
    )
    pieces = lax.all_to_all(partial_sum, "sta", 0, 0, tiled=True)
    return jnp.sum(pieces, axis=0)[:, None, :]


def solution(mesh):
    placed = (P("sta", None, "tm"), P("tm", None, "sta", None, None), P(), P(None, None, "sta"))
    return jax.shard_map(
        shards, mesh=mesh, in_specs=placed, out_specs=P(None, "sta", "tm"), check_vma=False
    )
```

```python
import jax
import jax.numpy as jnp
from jax import lax
from jax.experimental import pallas as pl
from jax.experimental.pallas import tpu as pltpu
from jax.sharding import PartitionSpec as P


STEP = 40
LANES = 128
WIN = 640

eps = 1e-06

VMEM = pl.BlockSpec(memory_space=pltpu.VMEM)
HBM = pl.BlockSpec(memory_space=pltpu.HBM)
LIMIT = pltpu.CompilerParams(vmem_limit_bytes=16 * 1024 * 1024)


def passed_along(block, axis, distance):
    devices = range(lax.axis_size(axis))
    route = [(i - distance, i) for i in devices if i - distance in devices]
    return lax.ppermute(block, axis, route)


def roll_left(value, amount):
    return pltpu.roll(value, value.shape[1] - amount, 1)


def turn(value, source):
    return jnp.take_along_axis(value, source & 127, axis=1, mode="promise_in_bounds")


def pack_kernel(bank_hbm, data_hbm, owners_hbm, lags_hbm, out_ref, data_ref, owners_ref, lags_ref, bank_ref, given_ref, wide_ref, sems):
    moves = [
        pltpu.make_async_copy(bank_hbm, bank_ref, sems.at[0]),
        pltpu.make_async_copy(data_hbm, data_ref, sems.at[1]),
        pltpu.make_async_copy(owners_hbm, given_ref, sems.at[2]),
        pltpu.make_async_copy(lags_hbm, lags_ref, sems.at[3]),
    ]
    for move in moves:
        move.start()
    tmpl_count, comp_count, local_sta, span_len = bank_ref.shape
    groups = out_ref.shape[0] // (tmpl_count * local_sta)
    rows = tmpl_count * local_sta
    lag = lax.broadcasted_iota(jnp.int32, (span_len, 1), 0)
    target = (lag // STEP) * LANES + lag % STEP
    lane = lax.broadcasted_iota(jnp.int32, (span_len, groups * LANES), 1)
    places = [
        jnp.where(lane == target + comp * STEP, 1.0, 0.0).astype(jnp.bfloat16) for comp in range(comp_count)
    ]
    moves[0].wait()
    packed = None
    for comp in range(comp_count):
        taps = bank_ref[:, comp].astype(jnp.float32).reshape(rows, span_len).astype(jnp.bfloat16)
        placed = jnp.dot(taps, places[comp], preferred_element_type=jnp.float32)
        packed = placed if packed is None else packed + placed
    for group in range(groups):
        wide_ref[pl.ds(group, rows, stride=groups), :] = packed[:, group * LANES : (group + 1) * LANES]
    out_ref[...] = wide_ref[...].astype(jnp.bfloat16)
    moves[2].wait()
    for b in range(owners_ref.shape[0]):
        owners_ref[b] = jnp.broadcast_to(given_ref[:, b : b + 1], owners_ref.shape[1:])
    moves[1].wait()
    moves[3].wait()


def pack(bank, data, owners, lags):
    tmpl_count, _, local_sta, span_len = bank.shape
    rows = local_sta * tmpl_count * -(-span_len // STEP)
    return pl.pallas_call(
        pack_kernel,
        out_shape=(
            jax.ShapeDtypeStruct((rows, LANES), jnp.bfloat16),
            jax.ShapeDtypeStruct(data.shape, data.dtype),
            jax.ShapeDtypeStruct((owners.shape[1], 8, LANES), jnp.int32),
            jax.ShapeDtypeStruct(lags.shape, lags.dtype),
        ),
        in_specs=[HBM] * 4,
        out_specs=(VMEM,) * 4,
        scratch_shapes=[
            pltpu.VMEM(bank.shape, bank.dtype),
            pltpu.VMEM(owners.shape, owners.dtype),
            pltpu.VMEM((rows, LANES), jnp.float32),
            pltpu.SemaphoreType.DMA((4,)),
        ],
        compiler_params=LIMIT,
        name="pack",
        cost_estimate=pl.CostEstimate(flops=40_000_000, bytes_accessed=200_000, transcendentals=0),
    )(*(pltpu.with_memory_space_constraint(x, pltpu.HBM) for x in (bank, data, owners, lags)))


def pick_kernel(owners_ref, seen_ref, out_ref):
    seen = seen_ref[...].astype(jnp.float32)
    _, groups, _ = seen.shape
    block = lax.broadcasted_iota(jnp.int32, seen.shape, 0)
    rows = []
    for b in range(owners_ref.shape[0]):
        chosen = block == owners_ref[b, :groups, :][None]
        rows.append(jnp.sum(jnp.where(chosen, seen, 0.0), axis=0))
    chunk = jnp.concatenate(rows, axis=0).astype(out_ref.dtype)
    out_ref[...] = jnp.broadcast_to(chunk[None], out_ref.shape)


def pick(owners, seen):
    blocks, groups, lanes = seen.shape
    return pl.pallas_call(
        pick_kernel,
        out_shape=jax.ShapeDtypeStruct((blocks, owners.shape[0] * groups, lanes), seen.dtype),
        in_specs=[VMEM, VMEM],
        out_specs=VMEM,
        compiler_params=LIMIT,
        name="pick",
        cost_estimate=pl.CostEstimate(flops=100_000, bytes_accessed=200_000, transcendentals=0),
    )(owners, seen)


def records_kernel(span_len, data_ref, edge_ref, hankel_ref, scale_ref):
    comp_count, local_sta, stretch_len = data_ref.shape
    tiles = WIN // 128
    squares = jnp.zeros((local_sta, WIN), jnp.float32)
    windows = []
    for comp in range(comp_count):
        edge = edge_ref[comp, :, : WIN - stretch_len]
        record = jnp.concatenate([data_ref[comp].astype(jnp.float32), edge.astype(jnp.float32)], axis=1)
        squares += record * record
        windows.append(record)
    row = lax.broadcasted_iota(jnp.int32, (STEP, 128), 0)
    lane = lax.broadcasted_iota(jnp.int32, (STEP, 128), 1)
    spare = jnp.zeros((LANES - comp_count * STEP, 128), jnp.float32)
    for sta in range(local_sta):
        turned = []
        for comp in range(comp_count):
            parts = []
            for tile in range(tiles):
                base = windows[comp][sta : sta + 1, tile * 128 : (tile + 1) * 128]
                parts.append(turn(jnp.broadcast_to(base, (STEP, 128)), lane + row))
            turned.append(parts)
        for tile in range(tiles):
            after = (tile + 1) % tiles
            block = [jnp.where(lane + row < 128, parts[tile], parts[after]) for parts in turned]
            hankel_ref[sta, :, tile * 128 : (tile + 1) * 128] = jnp.concatenate(block + [spare], axis=0).astype(jnp.bfloat16)
    run, total, at, width = squares, None, 0, 1
    while width <= span_len:
        if span_len & width:
            piece = run if at == 0 else roll_left(run, at)
            total = piece if total is None else total + piece
            at += width
        if 2 * width <= span_len:
            run = run + roll_left(run, width)
        width *= 2
    scale_ref[...] = 1.0 / jnp.sqrt(total / (comp_count * span_len) + eps)


def records(data, edge, span_len):
    _, local_sta, _ = data.shape
    return pl.pallas_call(
        lambda *refs: records_kernel(span_len, *refs),
        out_shape=(
            jax.ShapeDtypeStruct((local_sta, LANES, WIN), jnp.bfloat16),
            jax.ShapeDtypeStruct((local_sta, WIN), jnp.float32),
        ),
        in_specs=[VMEM, VMEM],
        out_specs=(VMEM, VMEM),
        compiler_params=LIMIT,
        name="records",
        cost_estimate=pl.CostEstimate(flops=8_000_000, bytes_accessed=4_000_000, transcendentals=4096),
    )(data, edge)


def stack_kernel(taps_count, tmpl_ref, hankel_ref, scale_ref, lag_ref, out_ref, wide_ref):
    tmpl_count, batch_count, stretch_len = out_ref.shape
    local_sta = hankel_ref.shape[0]
    groups = tmpl_ref.shape[1] // batch_count
    inner = batch_count * groups
    tiles = stretch_len // 128
    lane = lax.broadcasted_iota(jnp.int32, (batch_count * tmpl_count, 128), 1)
    wide_ref[...] = tmpl_ref[...].astype(jnp.float32).reshape(wide_ref.shape)
    total = None
    for sta in range(local_sta):
        taps = []
        for group in range(groups):
            for batch in range(batch_count):
                start = sta * inner + batch * groups + group
                taps.append(wide_ref[pl.ds(start, tmpl_count, stride=local_sta * inner), :])
        left = jnp.concatenate(taps, axis=0)
        rows = batch_count * tmpl_count
        power = sum(left[g * rows : (g + 1) * rows] * left[g * rows : (g + 1) * rows] for g in range(groups))
        power = jnp.sum(power, axis=1, keepdims=True) / taps_count
        prods = jnp.dot(left.astype(jnp.bfloat16), hankel_ref[sta], preferred_element_type=jnp.float32)
        prod = prods[:rows]
        for group in range(1, groups):
            prod += roll_left(prods[group * rows : (group + 1) * rows], group * STEP)
        scores = prod * (1.0 / (taps_count * jnp.sqrt(power + eps))) * scale_ref[sta : sta + 1, :]
        source = lane + lag_ref[:, sta : sta + 1]
        turned = [turn(scores[:, t * 128 : (t + 1) * 128], source) for t in range(tiles + 1)]
        shifted = [jnp.where(source < 128, turned[t], turned[t + 1]) for t in range(tiles)]
        total = shifted if total is None else [x + y for x, y in zip(total, shifted)]
    total = jnp.concatenate(total, axis=1)
    for batch in range(batch_count):
        out_ref[:, batch, :] = total[batch * tmpl_count : (batch + 1) * tmpl_count]


def stack(tmpl, hankel, scale, lags, taps_count, out_shape):
    return pl.pallas_call(
        lambda *refs: stack_kernel(taps_count, *refs),
        out_shape=jax.ShapeDtypeStruct(out_shape, jnp.float32),
        in_specs=[VMEM] * 4,
        out_specs=VMEM,
        scratch_shapes=[pltpu.VMEM((tmpl.shape[0] * tmpl.shape[1], LANES), jnp.float32)],
        compiler_params=LIMIT,
        name="stack",
        cost_estimate=pl.CostEstimate(flops=60_000_000, bytes_accessed=4_000_000, transcendentals=4096),
    )(tmpl, hankel, scale, lags)


def shards(data, bank, owners, moveouts):
    local_sta, comp_count, stretch_len = data.shape
    span_len = bank.shape[-1]
    tmpl_count = bank.shape[1]
    batch_count = owners.shape[0]
    blocks = lax.axis_size("tm")
    source = jnp.transpose(data, (1, 0, 2))
    lags = moveouts.reshape(batch_count * tmpl_count, local_sta)
    slot, series, owned, lags = pack(jnp.transpose(bank[0], (0, 2, 1, 3)), source, owners[None], lags)
    seen = lax.all_to_all(slot.reshape(blocks, -1, LANES), "tm", 0, 0, tiled=True)
    edge = passed_along(source, "tm", -1)
    chosen = pick(owned, seen)
    tmpl = lax.all_to_all(chosen, "tm", 0, 0, tiled=True)
    hankel, scale = records(series, edge, span_len)
    partial_sum = stack(
        tmpl, hankel, scale, lags, comp_count * span_len, (tmpl_count, batch_count, stretch_len)
    )
    pieces = lax.all_to_all(partial_sum, "sta", 0, 0, tiled=True)
    return jnp.sum(pieces, axis=0)[:, None, :]


def solution(mesh):
    placed = (P("sta", None, "tm"), P("tm", None, "sta", None, None), P(), P(None, None, "sta"))
    return jax.shard_map(
        shards, mesh=mesh, in_specs=placed, out_specs=P(None, "sta", "tm"), check_vma=False
    )
```

```python
import jax
import jax.numpy as jnp
from jax import lax
from jax.experimental import pallas as pl
from jax.experimental.pallas import tpu as pltpu
from jax.sharding import PartitionSpec as P


STEP = 40
LANES = 128
WIN = 640

eps = 1e-06

VMEM = pl.BlockSpec(memory_space=pltpu.VMEM)
HBM = pl.BlockSpec(memory_space=pltpu.HBM)
LIMIT = pltpu.CompilerParams(vmem_limit_bytes=16 * 1024 * 1024)


def passed_along(block, axis, distance):
    devices = range(lax.axis_size(axis))
    route = [(i - distance, i) for i in devices if i - distance in devices]
    return lax.ppermute(block, axis, route)


def roll_left(value, amount):
    return pltpu.roll(value, value.shape[1] - amount, 1)


def turn(value, source):
    return jnp.take_along_axis(value, source & 127, axis=1, mode="promise_in_bounds")


def load_kernel(data_hbm, owners_hbm, lags_hbm, data_ref, owners_ref, lags_ref, place_ref, given_ref, sems):
    moves = [
        pltpu.make_async_copy(owners_hbm, given_ref, sems.at[0]),
        pltpu.make_async_copy(data_hbm, data_ref, sems.at[1]),
        pltpu.make_async_copy(lags_hbm, lags_ref, sems.at[2]),
    ]
    for move in moves:
        move.start()
    comp_count, span_len, width = place_ref.shape
    lag = lax.broadcasted_iota(jnp.int32, (span_len, 1), 0)
    target = (lag // STEP) * LANES + lag % STEP
    lane = lax.broadcasted_iota(jnp.int32, (span_len, width), 1)
    for comp in range(comp_count):
        place_ref[comp] = jnp.where(lane == target + comp * STEP, 1.0, 0.0).astype(jnp.bfloat16)
    moves[0].wait()
    for b in range(owners_ref.shape[0]):
        owners_ref[b] = jnp.broadcast_to(given_ref[:, b : b + 1], owners_ref.shape[1:])
    moves[1].wait()
    moves[2].wait()


def load(data, owners, lags, span_len):
    given = [pltpu.with_memory_space_constraint(x, pltpu.HBM) for x in (data, owners, lags)]
    width = -(-span_len // STEP) * LANES
    return pl.pallas_call(
        load_kernel,
        out_shape=(
            jax.ShapeDtypeStruct(data.shape, data.dtype),
            jax.ShapeDtypeStruct((owners.shape[1], 8, LANES), jnp.int32),
            jax.ShapeDtypeStruct(lags.shape, lags.dtype),
            jax.ShapeDtypeStruct((data.shape[0], span_len, width), jnp.bfloat16),
        ),
        in_specs=[HBM] * 3,
        out_specs=(VMEM,) * 4,
        scratch_shapes=[pltpu.VMEM(owners.shape, owners.dtype), pltpu.SemaphoreType.DMA((3,))],
        compiler_params=LIMIT,
        name="load",
        cost_estimate=pl.CostEstimate(flops=500_000, bytes_accessed=500_000, transcendentals=0),
    )(*given)


def chosen_source(seen, source):
    block = lax.broadcasted_iota(jnp.int32, seen.shape, 0)
    return jnp.sum(jnp.where(block == source, seen, 0.0), axis=0)


def repack_kernel(owners_ref, seen_ref, place_ref, out_ref, wide_ref):
    peers, comp_count, local_sta, _ = seen_ref.shape
    batch_count = owners_ref.shape[0]
    groups = place_ref.shape[2] // LANES
    rows = batch_count * local_sta
    packed = None
    for comp in range(comp_count):
        taps = []
        for b in range(batch_count):
            owner = owners_ref[b, 0:1, 0:1] % peers
            taps.append(chosen_source(seen_ref[:, comp].astype(jnp.float32), owner[None]))
        taps = jnp.concatenate(taps, axis=0).astype(jnp.bfloat16)
        placed = jnp.dot(taps, place_ref[comp], preferred_element_type=jnp.float32)
        packed = placed if packed is None else packed + placed
    for group in range(groups):
        wide_ref[pl.ds(group, rows, stride=groups), :] = packed[:, group * LANES : (group + 1) * LANES]
    chunk = wide_ref[...].astype(out_ref.dtype)
    out_ref[...] = jnp.broadcast_to(chunk[None], out_ref.shape)


def repack(owners, seen, place, peers):
    batch_count = owners.shape[0]
    rows = batch_count * seen.shape[2] * (place.shape[2] // LANES)
    return pl.pallas_call(
        repack_kernel,
        out_shape=jax.ShapeDtypeStruct((peers, rows, LANES), seen.dtype),
        in_specs=[VMEM] * 3,
        out_specs=VMEM,
        scratch_shapes=[pltpu.VMEM((rows, LANES), jnp.float32)],
        compiler_params=LIMIT,
        name="repack",
        cost_estimate=pl.CostEstimate(flops=8_000_000, bytes_accessed=500_000, transcendentals=0),
    )(owners, seen, place)


def pick_kernel(inner, owners_ref, seen_ref, out_ref):
    batch_count = owners_ref.shape[0]
    rows = seen_ref.shape[1] // batch_count
    picked = []
    for b in range(batch_count):
        owner = owners_ref[b, 0:1, 0:1] // inner
        picked.append(chosen_source(seen_ref[:, b * rows : (b + 1) * rows].astype(jnp.float32), owner[None]))
    chunk = jnp.concatenate(picked, axis=0).astype(out_ref.dtype)
    out_ref[...] = jnp.broadcast_to(chunk[None], out_ref.shape)


def pick(owners, seen, inner):
    return pl.pallas_call(
        lambda *refs: pick_kernel(inner, *refs),
        out_shape=jax.ShapeDtypeStruct((inner,) + seen.shape[1:], seen.dtype),
        in_specs=[VMEM, VMEM],
        out_specs=VMEM,
        compiler_params=LIMIT,
        name="pick",
        cost_estimate=pl.CostEstimate(flops=100_000, bytes_accessed=200_000, transcendentals=0),
    )(owners, seen)


def records_kernel(span_len, data_ref, edge_ref, hankel_ref, scale_ref):
    comp_count, local_sta, stretch_len = data_ref.shape
    tiles = WIN // 128
    squares = jnp.zeros((local_sta, WIN), jnp.float32)
    windows = []
    for comp in range(comp_count):
        edge = edge_ref[comp, :, : WIN - stretch_len]
        record = jnp.concatenate([data_ref[comp].astype(jnp.float32), edge.astype(jnp.float32)], axis=1)
        squares += record * record
        windows.append(record)
    row = lax.broadcasted_iota(jnp.int32, (STEP, 128), 0)
    lane = lax.broadcasted_iota(jnp.int32, (STEP, 128), 1)
    spare = jnp.zeros((LANES - comp_count * STEP, 128), jnp.float32)
    for sta in range(local_sta):
        turned = []
        for comp in range(comp_count):
            parts = []
            for tile in range(tiles):
                base = windows[comp][sta : sta + 1, tile * 128 : (tile + 1) * 128]
                parts.append(turn(jnp.broadcast_to(base, (STEP, 128)), lane + row))
            turned.append(parts)
        for tile in range(tiles):
            after = (tile + 1) % tiles
            block = [jnp.where(lane + row < 128, parts[tile], parts[after]) for parts in turned]
            hankel_ref[sta, :, tile * 128 : (tile + 1) * 128] = jnp.concatenate(block + [spare], axis=0).astype(jnp.bfloat16)
    run, total, at, width = squares, None, 0, 1
    while width <= span_len:
        if span_len & width:
            piece = run if at == 0 else roll_left(run, at)
            total = piece if total is None else total + piece
            at += width
        if 2 * width <= span_len:
            run = run + roll_left(run, width)
        width *= 2
    scale_ref[...] = 1.0 / jnp.sqrt(total / (comp_count * span_len) + eps)


def records(data, edge, span_len):
    _, local_sta, _ = data.shape
    return pl.pallas_call(
        lambda *refs: records_kernel(span_len, *refs),
        out_shape=(
            jax.ShapeDtypeStruct((local_sta, LANES, WIN), jnp.bfloat16),
            jax.ShapeDtypeStruct((local_sta, WIN), jnp.float32),
        ),
        in_specs=[VMEM, VMEM],
        out_specs=(VMEM, VMEM),
        compiler_params=LIMIT,
        name="records",
        cost_estimate=pl.CostEstimate(flops=8_000_000, bytes_accessed=4_000_000, transcendentals=4096),
    )(data, edge)


def stack_kernel(taps_count, tmpl_ref, hankel_ref, scale_ref, lag_ref, out_ref, wide_ref):
    tmpl_count, batch_count, stretch_len = out_ref.shape
    local_sta = hankel_ref.shape[0]
    groups = tmpl_ref.shape[1] // (batch_count * local_sta)
    tiles = stretch_len // 128
    lane = lax.broadcasted_iota(jnp.int32, (batch_count * tmpl_count, 128), 1)
    wide_ref[...] = tmpl_ref[...].astype(jnp.float32).reshape(wide_ref.shape)
    total = None
    for sta in range(local_sta):
        taps = []
        for group in range(groups):
            for batch in range(batch_count):
                start = (batch * local_sta + sta) * groups + group
                taps.append(wide_ref[pl.ds(start, tmpl_count, stride=tmpl_ref.shape[1]), :])
        left = jnp.concatenate(taps, axis=0)
        rows = batch_count * tmpl_count
        power = sum(left[g * rows : (g + 1) * rows] * left[g * rows : (g + 1) * rows] for g in range(groups))
        power = jnp.sum(power, axis=1, keepdims=True) / taps_count
        prods = jnp.dot(left.astype(jnp.bfloat16), hankel_ref[sta], preferred_element_type=jnp.float32)
        prod = prods[:rows]
        for group in range(1, groups):
            prod += roll_left(prods[group * rows : (group + 1) * rows], group * STEP)
        scores = prod * (1.0 / (taps_count * jnp.sqrt(power + eps))) * scale_ref[sta : sta + 1, :]
        source = lane + lag_ref[:, sta : sta + 1]
        turned = [turn(scores[:, t * 128 : (t + 1) * 128], source) for t in range(tiles + 1)]
        shifted = [jnp.where(source < 128, turned[t], turned[t + 1]) for t in range(tiles)]
        total = shifted if total is None else [x + y for x, y in zip(total, shifted)]
    total = jnp.concatenate(total, axis=1)
    for batch in range(batch_count):
        out_ref[:, batch, :] = total[batch * tmpl_count : (batch + 1) * tmpl_count]


def stack(tmpl, hankel, scale, lags, taps_count, out_shape):
    return pl.pallas_call(
        lambda *refs: stack_kernel(taps_count, *refs),
        out_shape=jax.ShapeDtypeStruct(out_shape, jnp.float32),
        in_specs=[VMEM] * 4,
        out_specs=VMEM,
        scratch_shapes=[pltpu.VMEM((tmpl.shape[0] * tmpl.shape[1], LANES), jnp.float32)],
        compiler_params=LIMIT,
        name="stack",
        cost_estimate=pl.CostEstimate(flops=60_000_000, bytes_accessed=4_000_000, transcendentals=4096),
    )(tmpl, hankel, scale, lags)


def shards(data, bank, owners, moveouts):
    local_sta, comp_count, stretch_len = data.shape
    span_len = bank.shape[-1]
    tmpl_count = bank.shape[1]
    batch_count = owners.shape[0]
    outer = lax.axis_size("tm") // tmpl_count
    near = [[far * tmpl_count + i for i in range(tmpl_count)] for far in range(outer)]
    across = [[far * tmpl_count + i for far in range(outer)] for i in range(tmpl_count)]

    def exchange(value, groups):
        return lax.all_to_all(value, "tm", 0, 0, axis_index_groups=groups, tiled=True)

    source = jnp.transpose(data, (1, 0, 2))
    lags = moveouts.reshape(batch_count * tmpl_count, local_sta)
    seen = exchange(jnp.transpose(bank[0], (0, 2, 1, 3)), near)
    series, owned, lags, place = load(source, owners[None], lags, span_len)
    edge = passed_along(source, "tm", -1)
    seen = exchange(repack(owned, seen, place, outer), across)
    tmpl = exchange(pick(owned, seen, tmpl_count), near)
    hankel, scale = records(series, edge, span_len)
    partial_sum = stack(
        tmpl, hankel, scale, lags, comp_count * span_len, (tmpl_count, batch_count, stretch_len)
    )
    pieces = lax.all_to_all(partial_sum, "sta", 0, 0, tiled=True)
    return jnp.sum(pieces, axis=0)[:, None, :]


def solution(mesh):
    placed = (P("sta", None, "tm"), P("tm", None, "sta", None, None), P(), P(None, None, "sta"))
    return jax.shard_map(
        shards, mesh=mesh, in_specs=placed, out_specs=P(None, "sta", "tm"), check_vma=False
    )
```

```python
import jax
import jax.numpy as jnp
from jax import lax
from jax.experimental import pallas as pl
from jax.experimental.pallas import tpu as pltpu
from jax.sharding import Mesh, PartitionSpec as P

STEP = 40
LANES = 128

eps = 1e-06

VMEM = pl.BlockSpec(memory_space=pltpu.VMEM)
HBM = pl.BlockSpec(memory_space=pltpu.HBM)
LIMIT = pltpu.CompilerParams(vmem_limit_bytes=24 * 1024 * 1024)


def up_to(value, unit):
    return -(-value // unit) * unit


def turn(value, source):
    return jnp.take_along_axis(value, source & 127, axis=1, mode="promise_in_bounds")


def chosen_source(seen, source):
    block = lax.broadcasted_iota(jnp.int32, seen.shape, 0)
    return jnp.sum(jnp.where(block == source, seen, 0.0), axis=0)


def pack_kernel(bank_hbm, data_hbm, owners_hbm, lags_hbm, out_ref, owners_ref, lags_ref, bank_ref, data_ref, given_ref, wide_ref, sems):
    moves = [
        pltpu.make_async_copy(bank_hbm, bank_ref, sems.at[0]),
        pltpu.make_async_copy(data_hbm, data_ref, sems.at[1]),
        pltpu.make_async_copy(owners_hbm, given_ref, sems.at[2]),
        pltpu.make_async_copy(lags_hbm, lags_ref, sems.at[3]),
    ]
    for move in moves:
        move.start()
    tmpl_count, comp_count, local_sta, span_len = bank_ref.shape
    tiles = data_ref.shape[2] // LANES
    groups = up_to(span_len, STEP) // STEP
    rows = tmpl_count * local_sta
    height = wide_ref.shape[0] // local_sta
    lag = lax.broadcasted_iota(jnp.int32, (span_len, 1), 0)
    target = (lag // STEP) * LANES + lag % STEP
    lane = lax.broadcasted_iota(jnp.int32, (span_len, groups * LANES), 1)
    places = [
        jnp.where(lane == target + comp * STEP, 1.0, 0.0).astype(jnp.bfloat16) for comp in range(comp_count)
    ]
    for at in range(tmpl_count * groups + comp_count * tiles, height):
        wide_ref[pl.ds(at, local_sta, stride=height), :] = jnp.zeros((local_sta, LANES), jnp.float32)
    moves[0].wait()
    packed = None
    for comp in range(comp_count):
        taps = bank_ref[:, comp].astype(jnp.float32).reshape(rows, span_len).astype(jnp.bfloat16)
        placed = jnp.dot(taps, places[comp], preferred_element_type=jnp.float32)
        packed = placed if packed is None else packed + placed
    for tmpl in range(tmpl_count):
        for group in range(groups):
            piece = packed[tmpl * local_sta : (tmpl + 1) * local_sta, group * LANES : (group + 1) * LANES]
            wide_ref[pl.ds(tmpl * groups + group, local_sta, stride=height), :] = piece
    moves[1].wait()
    for comp in range(comp_count):
        for tile in range(tiles):
            piece = data_ref[comp, :, tile * LANES : (tile + 1) * LANES].astype(jnp.float32)
            at = tmpl_count * groups + comp * tiles + tile
            wide_ref[pl.ds(at, local_sta, stride=height), :] = piece
    out_ref[...] = wide_ref[...].astype(jnp.bfloat16)
    moves[2].wait()
    for b in range(owners_ref.shape[0]):
        owners_ref[b] = jnp.broadcast_to(given_ref[:, b : b + 1], owners_ref.shape[1:])
    moves[3].wait()


def pack(bank, data, owners, lags):
    tmpl_count, comp_count, local_sta, span_len = bank.shape
    groups = up_to(span_len, STEP) // STEP
    height = up_to(tmpl_count * groups + comp_count * data.shape[2] // LANES, 16)
    given = [pltpu.with_memory_space_constraint(x, pltpu.HBM) for x in (bank, data, owners, lags)]
    out, owned, own_lags = pl.pallas_call(
        pack_kernel,
        out_shape=(
            jax.ShapeDtypeStruct((local_sta * height, LANES), jnp.bfloat16),
            jax.ShapeDtypeStruct((owners.shape[1], 8, LANES), jnp.int32),
            jax.ShapeDtypeStruct(lags.shape, lags.dtype),
        ),
        in_specs=[HBM] * 4,
        out_specs=(VMEM,) * 3,
        scratch_shapes=[
            pltpu.VMEM(bank.shape, bank.dtype),
            pltpu.VMEM(data.shape, data.dtype),
            pltpu.VMEM(owners.shape, owners.dtype),
            pltpu.VMEM((local_sta * height, LANES), jnp.float32),
            pltpu.SemaphoreType.DMA((4,)),
        ],
        compiler_params=LIMIT,
        name="pack",
        cost_estimate=pl.CostEstimate(flops=40_000_000, bytes_accessed=200_000, transcendentals=0),
    )(*given)
    return out.reshape(local_sta, height, LANES), owned, own_lags


def forward_kernel(sizes, owners_ref, seen_ref, out_ref):
    template_rows, comp_count, tiles, edge_tiles = sizes
    peers = seen_ref.shape[0]
    seen = seen_ref[:, :template_rows].astype(jnp.float32)
    parts = []
    for b in range(owners_ref.shape[0]):
        parts.append(chosen_source(seen, (owners_ref[b, 0:1, 0:1] % peers)[None]))
    first = seen_ref[0].astype(jnp.float32)
    for comp in range(comp_count):
        at = template_rows + comp * tiles
        parts.append(first[at : at + edge_tiles])
    chunk = jnp.concatenate(parts, axis=0)
    rest = out_ref.shape[1] - chunk.shape[0]
    chunk = jnp.concatenate([chunk, jnp.zeros((rest, LANES), jnp.float32)], axis=0).astype(out_ref.dtype)
    out_ref[...] = jnp.broadcast_to(chunk[None], out_ref.shape)


def forward(owners, seen, peers, sizes):
    template_rows, comp_count, tiles, edge_tiles = sizes
    rows = up_to(owners.shape[0] * template_rows + comp_count * edge_tiles, 8)
    return pl.pallas_call(
        lambda *refs: forward_kernel(sizes, *refs),
        out_shape=jax.ShapeDtypeStruct((peers, rows, LANES), seen.dtype),
        in_specs=[VMEM] * 2,
        out_specs=VMEM,
        compiler_params=LIMIT,
        name="forward",
        cost_estimate=pl.CostEstimate(flops=1_000_000, bytes_accessed=500_000, transcendentals=0),
    )(owners, seen)


def stack_kernel(span_len, sizes, owners_ref, seen_ref, got_ref, lag_ref, out_ref, hankel_ref, tap_ref):
    template_rows, comp_count, tiles, edge_tiles = sizes
    blocks, tmpl_count, batch_count, stretch_len = out_ref.shape
    peers = got_ref.shape[0]
    groups = template_rows // tmpl_count
    rows = batch_count * tmpl_count
    taps_count = comp_count * span_len
    body = blocks * tiles
    held = body + edge_tiles
    near, far = lax.axis_index("near"), lax.axis_index("far")

    at = batch_count * template_rows
    edge = chosen_source(got_ref[:, at:].astype(jnp.float32), far + 1)
    row = lax.broadcasted_iota(jnp.int32, (STEP, LANES), 0)
    lane = lax.broadcasted_iota(jnp.int32, (STEP, LANES), 1)
    spare = jnp.zeros((LANES - comp_count * STEP, LANES), jnp.float32)
    samples = []
    for comp in range(comp_count):
        for_comp = []
        for block in range(blocks):
            at = template_rows + comp * tiles
            for_comp.append(seen_ref[block, at : at + tiles].astype(jnp.float32))
        for_comp.append(edge[comp * edge_tiles : (comp + 1) * edge_tiles])
        samples.append(for_comp)

    def sample_row(comp, tile):
        block, within = (tile // tiles, tile % tiles) if tile < body else (blocks, tile - body)
        return samples[comp][block][within : within + 1]

    later = None
    for tile in range(held - 1, -1, -1):
        turned = [
            turn(jnp.broadcast_to(sample_row(comp, tile), (STEP, LANES)), lane + row) for comp in range(comp_count)
        ]
        block = [
            jnp.where(lane + row < LANES, turned[comp], 0.0 if later is None else later[comp])
            for comp in range(comp_count)
        ]
        hankel_ref[:, tile * LANES : (tile + 1) * LANES] = jnp.concatenate(block + [spare], axis=0).astype(jnp.bfloat16)
        later = turned

    height = up_to(held + 1, 8)
    squares = None
    for comp in range(comp_count):
        series = jnp.concatenate(
            samples[comp] + [jnp.zeros((height - held, LANES), jnp.float32)], axis=0
        )
        squares = series * series if squares is None else squares + series * series
    wide_lane = lax.broadcasted_iota(jnp.int32, (height, LANES), 1)

    def ahead(value, amount):
        if amount >= LANES:
            value, amount = pltpu.roll(value, height - 1, 0), amount - LANES
        if amount == 0:
            return value
        value = pltpu.roll(value, LANES - amount, 1)
        return jnp.where(wide_lane < LANES - amount, value, pltpu.roll(value, height - 1, 0))

    run, total, at, width = squares, None, 0, 1
    while width <= span_len:
        if span_len & width:
            piece = ahead(run, at)
            total = piece if total is None else total + piece
            at += width
        if 2 * width <= span_len:
            run = run + ahead(run, width)
        width *= 2
    scale = 1.0 / jnp.sqrt(total / taps_count + eps)

    for b in range(batch_count):
        got = got_ref[:, b * template_rows : (b + 1) * template_rows].astype(jnp.float32)
        source = owners_ref[b, 0:1, 0:1] // seen_ref.shape[0]
        tap_ref[b * template_rows : (b + 1) * template_rows, :] = chosen_source(got, source[None])
    taps = []
    for group in range(groups):
        for b in range(batch_count):
            taps.append(tap_ref[pl.ds(b * template_rows + group, tmpl_count, stride=groups), :])
    left = jnp.concatenate(taps, axis=0)
    power = sum(left[g * rows : (g + 1) * rows] * left[g * rows : (g + 1) * rows] for g in range(groups))
    power = jnp.sum(power, axis=1, keepdims=True) / taps_count
    gain = 1.0 / (taps_count * jnp.sqrt(power + eps))
    left = left.astype(jnp.bfloat16)

    station = lax.broadcasted_iota(jnp.int32, lag_ref.shape, 1)
    lags = jnp.sum(jnp.where(station == near, lag_ref[...], 0), axis=1, keepdims=True)
    step = lax.broadcasted_iota(jnp.int32, (rows, LANES), 1)
    source = step + lags
    after, after_scores = None, None
    for tile in range(held - 1, -1, -1):
        prods = jnp.dot(left, hankel_ref[:, tile * LANES : (tile + 1) * LANES], preferred_element_type=jnp.float32)
        turned = [prods[:rows]]
        for group in range(1, groups):
            turned.append(pltpu.roll(prods[group * rows : (group + 1) * rows], LANES - group * STEP, 1))
        if tile <= body:
            prod = turned[0]
            for group in range(1, groups):
                prod += jnp.where(step < LANES - group * STEP, turned[group], after[group])
            scores = turn(prod * gain * scale[tile : tile + 1], source)
            if tile < body:
                shifted = jnp.where(source < LANES, scores, after_scores)
                block, within = tile // tiles, tile % tiles
                for b in range(batch_count):
                    out_ref[block, :, b, within * LANES : (within + 1) * LANES] = shifted[b * tmpl_count : (b + 1) * tmpl_count]
            after_scores = scores
        after = turned


def stack(owners, seen, got, lags, span_len, sizes, out_shape):
    template_rows, comp_count, tiles, edge_tiles = sizes
    held = out_shape[0] * tiles + edge_tiles
    return pl.pallas_call(
        lambda *refs: stack_kernel(span_len, sizes, *refs),
        out_shape=jax.ShapeDtypeStruct(out_shape, jnp.float32),
        in_specs=[VMEM] * 4,
        out_specs=VMEM,
        scratch_shapes=[
            pltpu.VMEM((LANES, held * LANES), jnp.bfloat16),
            pltpu.VMEM((owners.shape[0] * template_rows, LANES), jnp.float32),
        ],
        compiler_params=LIMIT,
        name="stack",
        cost_estimate=pl.CostEstimate(flops=60_000_000, bytes_accessed=2_000_000, transcendentals=4096),
    )(owners, seen, got, lags)


def shards(data, bank, owners, moveouts):
    local_sta, comp_count, stretch_len = data.shape
    span_len = bank.shape[-1]
    tmpl_count = bank.shape[1]
    batch_count = owners.shape[0]
    far, near, groups = lax.axis_size("far"), lax.axis_size("near"), lax.axis_size("sta")
    tiles = stretch_len // LANES
    template_rows = tmpl_count * (up_to(span_len, STEP) // STEP)
    sizes = (template_rows, comp_count, tiles, 2)

    def exchange(value, axis):
        return lax.all_to_all(value, axis, 0, 0, tiled=True)

    lags = moveouts.reshape(batch_count * tmpl_count, local_sta)
    slot, owned, lags = pack(jnp.transpose(bank[0], (0, 2, 1, 3)), jnp.transpose(data, (1, 0, 2)), owners[None], lags)
    seen = exchange(slot, "near")
    got = exchange(forward(owned, seen, far, sizes), "far")
    scores = stack(owned, seen, got, lags, span_len, sizes, (near, tmpl_count, batch_count, stretch_len))
    pieces = exchange(scores.reshape(near * groups, batch_count, stretch_len), ("near", "sta"))
    return jnp.sum(pieces, axis=0)[:, None, :]


def solution(mesh):
    blocks, groups = mesh.devices.shape
    near = groups
    split = Mesh(mesh.devices.reshape(blocks // near, near, groups), ("far", "near", "sta"))
    time = ("far", "near")
    placed = (P("sta", None, time), P(time, None, "sta", None, None), P(), P(None, None, "sta"))
    return jax.shard_map(
        shards, mesh=split, in_specs=placed, out_specs=P(None, "sta", time), check_vma=False
    )
```

```python
import jax
import jax.numpy as jnp
from jax import lax
from jax.experimental import pallas as pl
from jax.experimental.pallas import tpu as pltpu
from jax.sharding import Mesh, PartitionSpec as P

STEP = 40
LANES = 128

eps = 1e-06

VMEM = pl.BlockSpec(memory_space=pltpu.VMEM)
HBM = pl.BlockSpec(memory_space=pltpu.HBM)
LIMIT = pltpu.CompilerParams(vmem_limit_bytes=24 * 1024 * 1024)


def up_to(value, unit):
    return -(-value // unit) * unit


def turn(value, source):
    return jnp.take_along_axis(value, source & 127, axis=1, mode="promise_in_bounds")


def chosen_source(seen, source):
    block = lax.broadcasted_iota(jnp.int32, seen.shape, 0)
    return jnp.sum(jnp.where(block == source, seen, 0.0), axis=0)


def pack_kernel(halves, bank_hbm, data_hbm, owners_hbm, lags_hbm, out_ref, owners_ref, lags_ref, bank_ref, data_ref, given_ref, wide_ref, sems):
    moves = [
        pltpu.make_async_copy(bank_hbm, bank_ref, sems.at[0]),
        pltpu.make_async_copy(data_hbm, data_ref, sems.at[1]),
        pltpu.make_async_copy(owners_hbm, given_ref, sems.at[2]),
        pltpu.make_async_copy(lags_hbm, lags_ref, sems.at[3]),
    ]
    for move in reversed(moves):
        move.start()
    tmpl_count, comp_count, local_sta, span_len = bank_ref.shape
    tiles = data_ref.shape[2] // LANES
    groups = up_to(span_len, STEP) // STEP
    rows = tmpl_count * local_sta
    height = wide_ref.shape[0] // (local_sta * halves)
    share = tmpl_count // halves
    batch_count = owners_ref.shape[0]

    def put(half, at, value):
        wide_ref[pl.ds(half * height + at, local_sta, stride=halves * height), :] = value

    lag = lax.broadcasted_iota(jnp.int32, (span_len, 1), 0)
    target = (lag // STEP) * LANES + lag % STEP
    lane = lax.broadcasted_iota(jnp.int32, (span_len, groups * LANES), 1)
    places = [
        jnp.where(lane == target + comp * STEP, 1.0, 0.0).astype(jnp.bfloat16) for comp in range(comp_count)
    ]
    for half in range(halves):
        for at in range(share * groups + comp_count * tiles + 1, height):
            put(half, at, jnp.zeros((local_sta, LANES), jnp.float32))
    moves[3].wait()
    given_row = lax.broadcasted_iota(jnp.int32, (batch_count * tmpl_count, LANES), 0)
    given_lane = lax.broadcasted_iota(jnp.int32, (batch_count * tmpl_count, LANES), 1)
    for half in range(halves):
        wanted = (given_lane // share) * tmpl_count + given_lane % share * halves + half
        spread = jnp.where(given_row == wanted, 1.0, 0.0).astype(jnp.bfloat16)
        delays = lax.dot_general(
            lags_ref[...].astype(jnp.bfloat16), spread, (((0,), (0,)), ((), ())), preferred_element_type=jnp.float32
        )
        put(half, share * groups + comp_count * tiles, delays)
    moves[2].wait()
    for b in range(owners_ref.shape[0]):
        owners_ref[b] = jnp.broadcast_to(given_ref[:, b : b + 1], owners_ref.shape[1:])
    moves[0].wait()
    packed = None
    for comp in range(comp_count):
        taps = bank_ref[:, comp].astype(jnp.float32).reshape(rows, span_len).astype(jnp.bfloat16)
        placed = jnp.dot(taps, places[comp], preferred_element_type=jnp.float32)
        packed = placed if packed is None else packed + placed
    for tmpl in range(tmpl_count):
        for group in range(groups):
            piece = packed[tmpl * local_sta : (tmpl + 1) * local_sta, group * LANES : (group + 1) * LANES]
            put(tmpl % halves, tmpl // halves * groups + group, piece)
    moves[1].wait()
    for comp in range(comp_count):
        for tile in range(tiles):
            piece = data_ref[comp, :, tile * LANES : (tile + 1) * LANES].astype(jnp.float32)
            for half in range(halves):
                put(half, share * groups + comp * tiles + tile, piece)
    out_ref[...] = wide_ref[...].astype(jnp.bfloat16)


def pack(bank, data, owners, lags, halves):
    tmpl_count, comp_count, local_sta, span_len = bank.shape
    groups = up_to(span_len, STEP) // STEP
    height = up_to(tmpl_count // halves * groups + comp_count * data.shape[2] // LANES + 1, 8)
    blocks = local_sta * halves
    given = [pltpu.with_memory_space_constraint(x, pltpu.HBM) for x in (bank, data, owners, lags)]
    out, owned = pl.pallas_call(
        lambda *refs: pack_kernel(halves, *refs),
        out_shape=(
            jax.ShapeDtypeStruct((blocks * height, LANES), jnp.bfloat16),
            jax.ShapeDtypeStruct((owners.shape[1], 8, LANES), jnp.int32),
        ),
        in_specs=[HBM] * 4,
        out_specs=(VMEM,) * 2,
        scratch_shapes=[
            pltpu.VMEM(lags.shape, lags.dtype),
            pltpu.VMEM(bank.shape, bank.dtype),
            pltpu.VMEM(data.shape, data.dtype),
            pltpu.VMEM(owners.shape, owners.dtype),
            pltpu.VMEM((blocks * height, LANES), jnp.float32),
            pltpu.SemaphoreType.DMA((4,)),
        ],
        compiler_params=LIMIT,
        name="pack",
        cost_estimate=pl.CostEstimate(flops=40_000_000, bytes_accessed=200_000, transcendentals=0),
    )(*given)
    return out.reshape(blocks, height, LANES), owned


def forward_kernel(sizes, owners_ref, seen_ref, out_ref):
    template_rows, comp_count, tiles, edge_tiles, halves = sizes
    peers = seen_ref.shape[0] // halves
    seen = seen_ref[:, :template_rows].astype(jnp.float32)
    parts = []
    for b in range(owners_ref.shape[0]):
        for half in range(halves):
            parts.append(chosen_source(seen, (owners_ref[b, 0:1, 0:1] % peers * halves + half)[None]))
    for half in range(halves):
        first = seen_ref[half].astype(jnp.float32)
        for comp in range(comp_count):
            at = template_rows + comp * tiles
            parts.append(first[at : at + edge_tiles])
    chunk = jnp.concatenate(parts, axis=0)
    rest = out_ref.shape[1] - chunk.shape[0]
    chunk = jnp.concatenate([chunk, jnp.zeros((rest, LANES), jnp.float32)], axis=0).astype(out_ref.dtype)
    out_ref[...] = jnp.broadcast_to(chunk[None], out_ref.shape)


def forward(owners, seen, peers, sizes):
    template_rows, comp_count, tiles, edge_tiles, halves = sizes
    rows = up_to(halves * (owners.shape[0] * template_rows + comp_count * edge_tiles), 8)
    return pl.pallas_call(
        lambda *refs: forward_kernel(sizes, *refs),
        out_shape=jax.ShapeDtypeStruct((peers, rows, LANES), seen.dtype),
        in_specs=[VMEM] * 2,
        out_specs=VMEM,
        compiler_params=LIMIT,
        name="forward",
        cost_estimate=pl.CostEstimate(flops=1_000_000, bytes_accessed=500_000, transcendentals=0),
    )(owners, seen)


def stack_kernel(span_len, sizes, owners_ref, seen_ref, got_ref, out_ref, hankel_ref, tap_ref, score_ref):
    template_rows, comp_count, tiles, edge_tiles, halves = sizes
    blocks, tmpl_count, batch_count, stretch_len = out_ref.shape
    groups = template_rows // tmpl_count
    rows = batch_count * tmpl_count
    taps_count = comp_count * span_len
    body = blocks * tiles
    held = body + edge_tiles
    at = halves * batch_count * template_rows
    edges = chosen_source(got_ref[:, at:].astype(jnp.float32), lax.axis_index("far") + 1)
    def station_samples(half):
        samples = []
        for comp in range(comp_count):
            at = template_rows + comp * tiles
            parts = [seen_ref[block * halves + half, at : at + tiles].astype(jnp.float32) for block in range(blocks)]
            at = (half * comp_count + comp) * edge_tiles
            samples.append(parts + [edges[at : at + edge_tiles]])
        return samples

    def build_hankel(all_samples):
        for half in range(halves):
            hankel_ref[half, comp_count * STEP :, :] = jnp.zeros((LANES - comp_count * STEP, held * LANES), jnp.bfloat16)
        row = lax.broadcasted_iota(jnp.int32, (8, LANES), 0)
        lane = lax.broadcasted_iota(jnp.int32, (8, LANES), 1)
        for lag in range(0, STEP, 8):
            source = lane + row + lag
            for half in range(halves):
                for comp in range(comp_count):
                    at, later = comp * STEP + lag, 0.0
                    for tile in range(held - 1, -1, -1):
                        block, within = (tile // tiles, tile % tiles) if tile < body else (blocks, tile - body)
                        base = all_samples[half][comp][block][within : within + 1]
                        turned = turn(jnp.broadcast_to(base, (8, LANES)), source)
                        value = jnp.where(source < LANES, turned, later).astype(jnp.bfloat16)
                        hankel_ref[half, at : at + 8, tile * LANES : (tile + 1) * LANES] = value
                        later = turned

    height = up_to(held + 1, 8)

    def inverse_energy(all_samples):
        rows = []
        for samples in all_samples:
            squares = None
            for comp in range(comp_count):
                series = jnp.concatenate(samples[comp] + [jnp.zeros((height - held, LANES), jnp.float32)], axis=0)
                squares = series * series if squares is None else squares + series * series
            rows.append(squares)
        first = jnp.concatenate(rows, axis=0)
        total_rows = first.shape[0]
        reach = up_to(LANES + span_len, LANES) // LANES
        sides = [first] + [pltpu.roll(first, total_rows - side, 0) for side in range(1, reach)]
        wide = jnp.concatenate(sides, axis=1)

        def ahead(value, amount):
            return pltpu.roll(value, reach * LANES - amount, 1)[:, : value.shape[1]] if amount else value

        sums, width = {1: wide}, 1
        for factor in (2, 2, 4, 4):
            last = sums[1] if width <= 2 else sums[width]
            unit = 1 if width <= 2 else width
            count = width * factor // unit
            total = last
            for part in range(1, count):
                total = total + ahead(last, part * unit)
            width *= factor
            sums[width] = total
        total, at = None, 0
        for width in sorted(sums, reverse=True):
            while span_len - at >= width:
                piece = ahead(sums[width], at)[:, :LANES]
                total = piece if total is None else total + piece
                at += width
        scale = 1.0 / jnp.sqrt(total / taps_count + eps)
        return [scale[i * height : (i + 1) * height] for i in range(len(all_samples))]

    for b in range(batch_count):
        at = b * halves * template_rows
        got = got_ref[:, at : at + halves * template_rows].astype(jnp.float32)
        source = owners_ref[b, 0:1, 0:1] // blocks
        tap_ref[at : at + halves * template_rows, :] = chosen_source(got, source[None])
    step = lax.broadcasted_iota(jnp.int32, (rows, LANES), 1)
    slot = lax.broadcasted_iota(jnp.int32, (rows, LANES), 0)
    lefts, gains, sources = [], [], []
    all_samples = [station_samples(half) for half in range(halves)]
    scales = inverse_energy(all_samples)
    build_hankel(all_samples)
    for half in range(halves):
        taps = []
        for group in range(groups):
            for b in range(batch_count):
                start = (b * halves + half) * template_rows + group
                taps.append(tap_ref[pl.ds(start, tmpl_count, stride=groups), :])
        left = jnp.concatenate(taps, axis=0)
        power = sum(left[g * rows : (g + 1) * rows] * left[g * rows : (g + 1) * rows] for g in range(groups))
        power = jnp.sum(power, axis=1, keepdims=True) / taps_count
        gains.append(1.0 / (taps_count * jnp.sqrt(power + eps)))
        lefts.append(left.astype(jnp.bfloat16))
        at = template_rows + comp_count * tiles
        delays = jnp.broadcast_to(seen_ref[half, at : at + 1].astype(jnp.float32), (rows, LANES))
        lags = jnp.sum(jnp.where(step == slot, delays, 0.0), axis=1, keepdims=True)
        sources.append(step + lags.astype(jnp.int32))
    for half in range(halves):
        prods = jnp.dot(lefts[half], hankel_ref[half], preferred_element_type=jnp.float32)
        after = None
        for tile in range(held - 1, -1, -1):
            at = tile * LANES
            turned = [prods[:rows, at : at + LANES]]
            for group in range(1, groups):
                part = prods[group * rows : (group + 1) * rows, at : at + LANES]
                turned.append(pltpu.roll(part, LANES - group * STEP, 1))
            if tile <= body:
                prod = turned[0]
                for group in range(1, groups):
                    prod += jnp.where(step < LANES - group * STEP, turned[group], after[group])
                score_ref[half, :, at : at + LANES] = prod * gains[half] * scales[half][tile : tile + 1]
            after = turned
    totals = [None] * body
    for half in range(halves):
        later = None
        for tile in range(body, -1, -1):
            scores = turn(score_ref[half, :, tile * LANES : (tile + 1) * LANES], sources[half])
            if tile < body:
                shifted = jnp.where(sources[half] < LANES, scores, later)
                totals[tile] = shifted if half == 0 else totals[tile] + shifted
            later = scores
    for tile in range(body):
        block, within = tile // tiles, tile % tiles
        for b in range(batch_count):
            part = totals[tile][b * tmpl_count : (b + 1) * tmpl_count]
            out_ref[block, :, b, within * LANES : (within + 1) * LANES] = part


def stack(owners, seen, got, span_len, sizes, out_shape):
    template_rows, comp_count, tiles, edge_tiles, halves = sizes
    held = out_shape[0] * tiles + edge_tiles
    return pl.pallas_call(
        lambda *refs: stack_kernel(span_len, sizes, *refs),
        out_shape=jax.ShapeDtypeStruct(out_shape, jnp.float32),
        in_specs=[VMEM] * 3,
        out_specs=VMEM,
        scratch_shapes=[
            pltpu.VMEM((halves, LANES, held * LANES), jnp.bfloat16),
            pltpu.VMEM((owners.shape[0] * halves * template_rows, LANES), jnp.float32),
            pltpu.VMEM((halves, out_shape[1] * out_shape[2], held * LANES), jnp.float32),
        ],
        compiler_params=LIMIT,
        name="stack",
        cost_estimate=pl.CostEstimate(flops=60_000_000, bytes_accessed=2_000_000, transcendentals=4096),
    )(owners, seen, got)


def shards(data, bank, owners, moveouts):
    local_sta, comp_count, stretch_len = data.shape
    span_len = bank.shape[-1]
    tmpl_count = bank.shape[1]
    batch_count = owners.shape[0]
    far, near, across, halves = (lax.axis_size(axis) for axis in ("far", "near", "across", "half"))
    tiles = stretch_len // LANES
    share = tmpl_count // halves
    sizes = (share * (up_to(span_len, STEP) // STEP), comp_count, tiles, 2, halves)

    def exchange(value, axis):
        return lax.all_to_all(value, axis, 0, 0, tiled=True)

    lags = moveouts.reshape(batch_count * tmpl_count, local_sta)
    slot, owned = pack(jnp.transpose(bank[0], (0, 2, 1, 3)), jnp.transpose(data, (1, 0, 2)), owners[None], lags, halves)
    seen = exchange(slot, ("near", "half"))
    got = exchange(forward(owned, seen, far, sizes), "far")
    scores = stack(owned, seen, got, span_len, sizes, (near, share, batch_count, stretch_len))
    pieces = exchange(scores.reshape(near * across, batch_count, stretch_len), ("near", "across"))
    return jnp.sum(pieces, axis=0)[:, None, :]


def solution(mesh):
    blocks, groups = mesh.devices.shape
    near, halves = 8, 2
    shape = (blocks // near, near, groups // halves, halves)
    split = Mesh(mesh.devices.reshape(shape), ("far", "near", "across", "half"))
    time, sta = ("far", "near"), ("across", "half")
    placed = (P(sta, None, time), P(time, None, sta, None, None), P(), P(None, None, sta))
    return jax.shard_map(
        shards, mesh=split, in_specs=placed, out_specs=P(None, sta, time), check_vma=False
    )
```

```python
import jax
import jax.numpy as jnp
from jax import lax
from jax.experimental import pallas as pl
from jax.experimental.pallas import tpu as pltpu
from jax.sharding import Mesh, PartitionSpec as P

STEP = 40
LANES = 128

eps = 1e-06

VMEM = pl.BlockSpec(memory_space=pltpu.VMEM)
HBM = pl.BlockSpec(memory_space=pltpu.HBM)
LIMIT = pltpu.CompilerParams(vmem_limit_bytes=24 * 1024 * 1024)


def up_to(value, unit):
    return -(-value // unit) * unit


def turn(value, source):
    return jnp.take_along_axis(value, source & 127, axis=1, mode="promise_in_bounds")


def chosen_source(seen, source):
    block = lax.broadcasted_iota(jnp.int32, seen.shape, 0)
    return jnp.sum(jnp.where(block == source, seen, 0.0), axis=0)


def pack_kernel(halves, bank_hbm, data_hbm, owners_hbm, lags_hbm, out_ref, owners_ref, lags_ref, bank_ref, data_ref, given_ref, wide_ref, sems):
    moves = [
        pltpu.make_async_copy(bank_hbm, bank_ref, sems.at[0]),
        pltpu.make_async_copy(data_hbm, data_ref, sems.at[1]),
        pltpu.make_async_copy(owners_hbm, given_ref, sems.at[2]),
        pltpu.make_async_copy(lags_hbm, lags_ref, sems.at[3]),
    ]
    for move in reversed(moves):
        move.start()
    tmpl_count, comp_count, local_sta, span_len = bank_ref.shape
    tiles = data_ref.shape[2] // LANES
    groups = up_to(span_len, STEP) // STEP
    rows = tmpl_count * local_sta
    height = wide_ref.shape[0] // (local_sta * halves)
    share = tmpl_count // halves
    batch_count = owners_ref.shape[0]

    def put(half, at, value):
        wide_ref[pl.ds(half * local_sta * height + at, local_sta, stride=height), :] = value

    lag = lax.broadcasted_iota(jnp.int32, (span_len, 1), 0)
    target = (lag // STEP) * LANES + lag % STEP
    lane = lax.broadcasted_iota(jnp.int32, (span_len, groups * LANES), 1)
    places = [
        jnp.where(lane == target + comp * STEP, 1.0, 0.0).astype(jnp.bfloat16) for comp in range(comp_count)
    ]
    for half in range(halves):
        for at in range(share * groups + comp_count * tiles + 1, height):
            put(half, at, jnp.zeros((local_sta, LANES), jnp.float32))
    moves[3].wait()
    given_row = lax.broadcasted_iota(jnp.int32, (batch_count * tmpl_count, LANES), 0)
    given_lane = lax.broadcasted_iota(jnp.int32, (batch_count * tmpl_count, LANES), 1)
    for half in range(halves):
        wanted = (given_lane // share) * tmpl_count + given_lane % share * halves + half
        spread = jnp.where(given_row == wanted, 1.0, 0.0).astype(jnp.bfloat16)
        delays = lax.dot_general(
            lags_ref[...].astype(jnp.bfloat16), spread, (((0,), (0,)), ((), ())), preferred_element_type=jnp.float32
        )
        put(half, share * groups + comp_count * tiles, delays)
    moves[2].wait()
    for b in range(owners_ref.shape[0]):
        owners_ref[b] = jnp.broadcast_to(given_ref[:, b : b + 1], owners_ref.shape[1:])
    moves[1].wait()
    for comp in range(comp_count):
        for tile in range(tiles):
            piece = data_ref[comp, :, tile * LANES : (tile + 1) * LANES].astype(jnp.float32)
            for half in range(halves):
                put(half, share * groups + comp * tiles + tile, piece)
    moves[0].wait()
    packed = None
    for comp in range(comp_count):
        taps = bank_ref[:, comp].astype(jnp.float32).reshape(rows, span_len).astype(jnp.bfloat16)
        placed = jnp.dot(taps, places[comp], preferred_element_type=jnp.float32)
        packed = placed if packed is None else packed + placed
    for tmpl in range(tmpl_count):
        for group in range(groups):
            piece = packed[tmpl * local_sta : (tmpl + 1) * local_sta, group * LANES : (group + 1) * LANES]
            put(tmpl % halves, tmpl // halves * groups + group, piece)
    out_ref[...] = wide_ref[...].astype(jnp.bfloat16)


def pack(bank, data, owners, lags, halves):
    tmpl_count, comp_count, local_sta, span_len = bank.shape
    groups = up_to(span_len, STEP) // STEP
    height = up_to(tmpl_count // halves * groups + comp_count * data.shape[2] // LANES + 1, 8)
    blocks = local_sta * halves
    given = [pltpu.with_memory_space_constraint(x, pltpu.HBM) for x in (bank, data, owners, lags)]
    out, owned = pl.pallas_call(
        lambda *refs: pack_kernel(halves, *refs),
        out_shape=(
            jax.ShapeDtypeStruct((blocks * height, LANES), jnp.bfloat16),
            jax.ShapeDtypeStruct((owners.shape[1], 8, LANES), jnp.int32),
        ),
        in_specs=[HBM] * 4,
        out_specs=(VMEM,) * 2,
        scratch_shapes=[
            pltpu.VMEM(lags.shape, lags.dtype),
            pltpu.VMEM(bank.shape, bank.dtype),
            pltpu.VMEM(data.shape, data.dtype),
            pltpu.VMEM(owners.shape, owners.dtype),
            pltpu.VMEM((blocks * height, LANES), jnp.float32),
            pltpu.SemaphoreType.DMA((4,)),
        ],
        compiler_params=LIMIT,
        name="pack",
        cost_estimate=pl.CostEstimate(flops=40_000_000, bytes_accessed=200_000, transcendentals=0),
    )(*given)
    return out.reshape(blocks, height, LANES), owned


def forward_kernel(sizes, owners_ref, seen_ref, out_ref):
    template_rows, comp_count, tiles, edge_tiles, halves = sizes
    peers = seen_ref.shape[0] // halves
    seen = seen_ref[:, :template_rows].astype(jnp.float32)
    parts = []
    for b in range(owners_ref.shape[0]):
        for half in range(halves):
            parts.append(chosen_source(seen, (owners_ref[b, 0:1, 0:1] % peers + half * peers)[None]))
    for half in range(halves):
        first = seen_ref[half * peers].astype(jnp.float32)
        for comp in range(comp_count):
            at = template_rows + comp * tiles
            parts.append(first[at : at + edge_tiles])
    chunk = jnp.concatenate(parts, axis=0)
    rest = out_ref.shape[1] - chunk.shape[0]
    chunk = jnp.concatenate([chunk, jnp.zeros((rest, LANES), jnp.float32)], axis=0).astype(out_ref.dtype)
    out_ref[...] = jnp.broadcast_to(chunk[None], out_ref.shape)


def forward(owners, seen, peers, sizes):
    template_rows, comp_count, tiles, edge_tiles, halves = sizes
    rows = up_to(halves * (owners.shape[0] * template_rows + comp_count * edge_tiles), 8)
    return pl.pallas_call(
        lambda *refs: forward_kernel(sizes, *refs),
        out_shape=jax.ShapeDtypeStruct((peers, rows, LANES), seen.dtype),
        in_specs=[VMEM] * 2,
        out_specs=VMEM,
        compiler_params=LIMIT,
        name="forward",
        cost_estimate=pl.CostEstimate(flops=1_000_000, bytes_accessed=500_000, transcendentals=0),
    )(owners, seen)


def stack_kernel(span_len, sizes, owners_ref, seen_ref, got_ref, out_ref, hankel_ref, tap_ref, score_ref):
    template_rows, comp_count, tiles, edge_tiles, halves = sizes
    tmpl_count, blocks, batch_count, stretch_len = out_ref.shape
    groups = template_rows // tmpl_count
    rows = batch_count * tmpl_count
    taps_count = comp_count * span_len
    body = blocks * tiles
    held = body + edge_tiles
    at = halves * batch_count * template_rows
    edges = chosen_source(got_ref[:, at:].astype(jnp.float32), lax.axis_index("far") + 1)
    def station_samples(half):
        samples = []
        for comp in range(comp_count):
            at = template_rows + comp * tiles
            parts = [seen_ref[half * blocks + block, at : at + tiles].astype(jnp.float32) for block in range(blocks)]
            at = (half * comp_count + comp) * edge_tiles
            samples.append(parts + [edges[at : at + edge_tiles]])
        return samples

    def build_hankel(all_samples):
        for half in range(halves):
            hankel_ref[half, comp_count * STEP :, :] = jnp.zeros((LANES - comp_count * STEP, held * LANES), jnp.bfloat16)
        row = lax.broadcasted_iota(jnp.int32, (8, LANES), 0)
        lane = lax.broadcasted_iota(jnp.int32, (8, LANES), 1)
        for lag in range(0, STEP, 8):
            source = lane + row + lag
            for half in range(halves):
                for comp in range(comp_count):
                    at, later = comp * STEP + lag, 0.0
                    for tile in range(held - 1, -1, -1):
                        block, within = (tile // tiles, tile % tiles) if tile < body else (blocks, tile - body)
                        base = all_samples[half][comp][block][within : within + 1]
                        turned = turn(jnp.broadcast_to(base, (8, LANES)), source)
                        value = jnp.where(source < LANES, turned, later).astype(jnp.bfloat16)
                        hankel_ref[half, at : at + 8, tile * LANES : (tile + 1) * LANES] = value
                        later = turned

    height = up_to(held + 1, 8)

    def inverse_energy(all_samples):
        rows = []
        for samples in all_samples:
            squares = None
            for comp in range(comp_count):
                series = jnp.concatenate(samples[comp] + [jnp.zeros((height - held, LANES), jnp.float32)], axis=0)
                squares = series * series if squares is None else squares + series * series
            rows.append(squares)
        first = jnp.concatenate(rows, axis=0)
        total_rows = first.shape[0]
        reach = up_to(LANES + span_len, LANES) // LANES
        sides = [first] + [pltpu.roll(first, total_rows - side, 0) for side in range(1, reach)]
        wide = jnp.concatenate(sides, axis=1)

        def ahead(value, amount):
            return pltpu.roll(value, reach * LANES - amount, 1)[:, : value.shape[1]] if amount else value

        sums, width = {1: wide}, 1
        while 2 * width <= min(span_len, LANES // 2):
            sums[2 * width] = sums[width] + ahead(sums[width], width)
            width *= 2
        total, at = None, 0
        for width in sorted(sums, reverse=True):
            while span_len - at >= width:
                piece = ahead(sums[width], at)[:, :LANES]
                total = piece if total is None else total + piece
                at += width
        scale = 1.0 / jnp.sqrt(total / taps_count + eps)
        return [scale[i * height : (i + 1) * height] for i in range(len(all_samples))]

    for b in range(batch_count):
        at = b * halves * template_rows
        got = got_ref[:, at : at + halves * template_rows].astype(jnp.float32)
        source = owners_ref[b, 0:1, 0:1] // blocks
        tap_ref[at : at + halves * template_rows, :] = chosen_source(got, source[None])
    step = lax.broadcasted_iota(jnp.int32, (rows, LANES), 1)
    slot = lax.broadcasted_iota(jnp.int32, (rows, LANES), 0)
    lefts, gains, sources = [], [], []
    all_samples = [station_samples(half) for half in range(halves)]
    scales = inverse_energy(all_samples)
    build_hankel(all_samples)
    for half in range(halves):
        taps = []
        for group in range(groups):
            for b in range(batch_count):
                start = (b * halves + half) * template_rows + group
                taps.append(tap_ref[pl.ds(start, tmpl_count, stride=groups), :])
        left = jnp.concatenate(taps, axis=0)
        power = sum(left[g * rows : (g + 1) * rows] * left[g * rows : (g + 1) * rows] for g in range(groups))
        power = jnp.sum(power, axis=1, keepdims=True) / taps_count
        gains.append(1.0 / (taps_count * jnp.sqrt(power + eps)))
        lefts.append(left.astype(jnp.bfloat16))
        at = template_rows + comp_count * tiles
        delays = jnp.broadcast_to(seen_ref[half * blocks, at : at + 1].astype(jnp.float32), (rows, LANES))
        lags = jnp.sum(jnp.where(step == slot, delays, 0.0), axis=1, keepdims=True)
        sources.append(step + lags.astype(jnp.int32))
    for half in range(halves):
        prods = jnp.dot(lefts[half], hankel_ref[half], preferred_element_type=jnp.float32)
        after = None
        for tile in range(held - 1, -1, -1):
            at = tile * LANES
            turned = [prods[:rows, at : at + LANES]]
            for group in range(1, groups):
                part = prods[group * rows : (group + 1) * rows, at : at + LANES]
                turned.append(pltpu.roll(part, LANES - group * STEP, 1))
            if tile <= body:
                prod = turned[0]
                for group in range(1, groups):
                    prod += jnp.where(step < LANES - group * STEP, turned[group], after[group])
                score_ref[half, :, at : at + LANES] = prod * gains[half] * scales[half][tile : tile + 1]
            after = turned
    totals = [None] * body
    for half in range(halves):
        later = None
        for tile in range(body, -1, -1):
            scores = turn(score_ref[half, :, tile * LANES : (tile + 1) * LANES], sources[half])
            if tile < body:
                shifted = jnp.where(sources[half] < LANES, scores, later)
                totals[tile] = shifted if half == 0 else totals[tile] + shifted
            later = scores
    for tile in range(body):
        block, within = tile // tiles, tile % tiles
        for b in range(batch_count):
            part = totals[tile][b * tmpl_count : (b + 1) * tmpl_count]
            out_ref[:, block, b, within * LANES : (within + 1) * LANES] = part


def stack(owners, seen, got, span_len, sizes, out_shape):
    template_rows, comp_count, tiles, edge_tiles, halves = sizes
    held = out_shape[1] * tiles + edge_tiles
    return pl.pallas_call(
        lambda *refs: stack_kernel(span_len, sizes, *refs),
        out_shape=jax.ShapeDtypeStruct(out_shape, jnp.float32),
        in_specs=[VMEM] * 3,
        out_specs=VMEM,
        scratch_shapes=[
            pltpu.VMEM((halves, LANES, held * LANES), jnp.bfloat16),
            pltpu.VMEM((owners.shape[0] * halves * template_rows, LANES), jnp.float32),
            pltpu.VMEM((halves, out_shape[0] * out_shape[2], held * LANES), jnp.float32),
        ],
        compiler_params=LIMIT,
        name="stack",
        cost_estimate=pl.CostEstimate(flops=60_000_000, bytes_accessed=2_000_000, transcendentals=4096),
    )(owners, seen, got)


def shards(data, bank, owners, moveouts):
    local_sta, comp_count, stretch_len = data.shape
    span_len = bank.shape[-1]
    tmpl_count = bank.shape[1]
    batch_count = owners.shape[0]
    far, near, across, halves = (lax.axis_size(axis) for axis in ("far", "near", "across", "half"))
    tiles = stretch_len // LANES
    share = tmpl_count // halves
    sizes = (share * (up_to(span_len, STEP) // STEP), comp_count, tiles, 2, halves)

    def exchange(value, axis):
        return lax.all_to_all(value, axis, 0, 0, tiled=True)

    lags = moveouts.reshape(batch_count * tmpl_count, local_sta)
    slot, owned = pack(jnp.transpose(bank[0], (0, 2, 1, 3)), jnp.transpose(data, (1, 0, 2)), owners[None], lags, halves)
    seen = exchange(slot, ("half", "near"))
    got = exchange(forward(owned, seen, far, sizes), "far")
    scores = stack(owned, seen, got, span_len, sizes, (share, near, batch_count, stretch_len))
    pieces = exchange(scores.reshape(near * across, batch_count, stretch_len), ("across", "near"))
    return jnp.sum(pieces, axis=0)[:, None, :]


def solution(mesh):
    blocks, groups = mesh.devices.shape
    near, halves = 8, 2
    shape = (blocks // near, near, groups // halves, halves)
    split = Mesh(mesh.devices.reshape(shape), ("far", "near", "across", "half"))
    time, sta = ("far", "near"), ("across", "half")
    placed = (P(sta, None, time), P(time, None, sta, None, None), P(), P(None, None, sta))
    return jax.shard_map(
        shards, mesh=split, in_specs=placed, out_specs=P(None, sta, time), check_vma=False
    )
```

```python
import jax
import jax.numpy as jnp
from jax import lax
from jax.experimental import pallas as pl
from jax.experimental.pallas import tpu as pltpu
from jax.sharding import Mesh, PartitionSpec as P

STEP = 40
LANES = 128

eps = 1e-06

VMEM = pl.BlockSpec(memory_space=pltpu.VMEM)
HBM = pl.BlockSpec(memory_space=pltpu.HBM)
LIMIT = pltpu.CompilerParams(vmem_limit_bytes=24 * 1024 * 1024)


def up_to(value, unit):
    return -(-value // unit) * unit


def turn(value, source):
    return jnp.take_along_axis(value, source & 127, axis=1, mode="promise_in_bounds")


def chosen_source(seen, source):
    block = lax.broadcasted_iota(jnp.int32, seen.shape, 0)
    return jnp.sum(jnp.where(block == source, seen, 0.0), axis=0)


def pack_kernel(halves, bank_hbm, data_hbm, owners_hbm, lags_hbm, out_ref, owners_ref, lags_ref, bank_ref, data_ref, given_ref, wide_ref, sems):
    moves = [
        None,
        pltpu.make_async_copy(data_hbm, data_ref, sems.at[1]),
        pltpu.make_async_copy(owners_hbm, given_ref, sems.at[2]),
        pltpu.make_async_copy(lags_hbm, lags_ref, sems.at[3]),
    ]
    pieces = [
        pltpu.make_async_copy(bank_hbm.at[:, comp], bank_ref.at[:, comp], sems.at[4 + comp])
        for comp in range(bank_ref.shape[1])
    ]
    for move in pieces + moves[:0:-1]:
        move.start()
    tmpl_count, comp_count, local_sta, span_len = bank_ref.shape
    tiles = data_ref.shape[2] // LANES
    groups = up_to(span_len, STEP) // STEP
    rows = tmpl_count * local_sta
    height = wide_ref.shape[0] // (local_sta * halves)
    share = tmpl_count // halves
    batch_count = owners_ref.shape[0]

    def put(half, at, value):
        wide_ref[pl.ds(half * local_sta * height + at, local_sta, stride=height), :] = value

    lag = lax.broadcasted_iota(jnp.int32, (span_len, 1), 0)
    target = (lag // STEP) * LANES + lag % STEP
    lane = lax.broadcasted_iota(jnp.int32, (span_len, groups * LANES), 1)
    places = [
        jnp.where(lane == target + comp * STEP, 1.0, 0.0).astype(jnp.bfloat16) for comp in range(comp_count)
    ]
    for half in range(halves):
        for at in range(share * groups + comp_count * tiles + 1, height):
            put(half, at, jnp.zeros((local_sta, LANES), jnp.float32))
    moves[3].wait()
    given_row = lax.broadcasted_iota(jnp.int32, (batch_count * tmpl_count, LANES), 0)
    given_lane = lax.broadcasted_iota(jnp.int32, (batch_count * tmpl_count, LANES), 1)
    for half in range(halves):
        wanted = (given_lane // share) * tmpl_count + given_lane % share * halves + half
        spread = jnp.where(given_row == wanted, 1.0, 0.0).astype(jnp.bfloat16)
        delays = lax.dot_general(
            lags_ref[...].astype(jnp.bfloat16), spread, (((0,), (0,)), ((), ())), preferred_element_type=jnp.float32
        )
        put(half, share * groups + comp_count * tiles, delays)
    moves[2].wait()
    for b in range(owners_ref.shape[0]):
        owners_ref[b] = jnp.broadcast_to(given_ref[:, b : b + 1], owners_ref.shape[1:])
    moves[1].wait()
    for comp in range(comp_count):
        for tile in range(tiles):
            piece = data_ref[comp, :, tile * LANES : (tile + 1) * LANES].astype(jnp.float32)
            for half in range(halves):
                put(half, share * groups + comp * tiles + tile, piece)
    packed = None
    for comp in range(comp_count):
        pieces[comp].wait()
        taps = bank_ref[:, comp].astype(jnp.float32).reshape(rows, span_len).astype(jnp.bfloat16)
        placed = jnp.dot(taps, places[comp], preferred_element_type=jnp.float32)
        packed = placed if packed is None else packed + placed
    for tmpl in range(tmpl_count):
        for group in range(groups):
            piece = packed[tmpl * local_sta : (tmpl + 1) * local_sta, group * LANES : (group + 1) * LANES]
            put(tmpl % halves, tmpl // halves * groups + group, piece)
    out_ref[...] = wide_ref[...].astype(jnp.bfloat16)


def pack(bank, data, owners, lags, halves):
    tmpl_count, comp_count, local_sta, span_len = bank.shape
    groups = up_to(span_len, STEP) // STEP
    height = up_to(tmpl_count // halves * groups + comp_count * data.shape[2] // LANES + 1, 8)
    blocks = local_sta * halves
    given = [pltpu.with_memory_space_constraint(x, pltpu.HBM) for x in (bank, data, owners, lags)]
    out, owned = pl.pallas_call(
        lambda *refs: pack_kernel(halves, *refs),
        out_shape=(
            jax.ShapeDtypeStruct((blocks * height, LANES), jnp.bfloat16),
            jax.ShapeDtypeStruct((owners.shape[1], 8, LANES), jnp.int32),
        ),
        in_specs=[HBM] * 4,
        out_specs=(VMEM,) * 2,
        scratch_shapes=[
            pltpu.VMEM(lags.shape, lags.dtype),
            pltpu.VMEM(bank.shape, bank.dtype),
            pltpu.VMEM(data.shape, data.dtype),
            pltpu.VMEM(owners.shape, owners.dtype),
            pltpu.VMEM((blocks * height, LANES), jnp.float32),
            pltpu.SemaphoreType.DMA((4 + comp_count,)),
        ],
        compiler_params=LIMIT,
        name="pack",
        cost_estimate=pl.CostEstimate(flops=40_000_000, bytes_accessed=200_000, transcendentals=0),
    )(*given)
    return out.reshape(blocks, height, LANES), owned


def forward_kernel(sizes, owners_ref, seen_ref, out_ref):
    template_rows, comp_count, tiles, edge_tiles, halves = sizes
    peers = seen_ref.shape[0] // halves
    seen = seen_ref[:, :template_rows].astype(jnp.float32)
    parts = []
    for b in range(owners_ref.shape[0]):
        for half in range(halves):
            parts.append(chosen_source(seen, (owners_ref[b, 0:1, 0:1] % peers + half * peers)[None]))
    for half in range(halves):
        first = seen_ref[half * peers].astype(jnp.float32)
        for comp in range(comp_count):
            at = template_rows + comp * tiles
            parts.append(first[at : at + edge_tiles])
    chunk = jnp.concatenate(parts, axis=0)
    rest = out_ref.shape[1] - chunk.shape[0]
    chunk = jnp.concatenate([chunk, jnp.zeros((rest, LANES), jnp.float32)], axis=0).astype(out_ref.dtype)
    out_ref[...] = jnp.broadcast_to(chunk[None], out_ref.shape)


def forward(owners, seen, peers, sizes):
    template_rows, comp_count, tiles, edge_tiles, halves = sizes
    rows = up_to(halves * (owners.shape[0] * template_rows + comp_count * edge_tiles), 8)
    return pl.pallas_call(
        lambda *refs: forward_kernel(sizes, *refs),
        out_shape=jax.ShapeDtypeStruct((peers, rows, LANES), seen.dtype),
        in_specs=[VMEM] * 2,
        out_specs=VMEM,
        compiler_params=LIMIT,
        name="forward",
        cost_estimate=pl.CostEstimate(flops=1_000_000, bytes_accessed=500_000, transcendentals=0),
    )(owners, seen)


def stack_kernel(span_len, sizes, owners_ref, seen_ref, got_ref, out_ref, hankel_ref, tap_ref, score_ref):
    template_rows, comp_count, tiles, edge_tiles, halves = sizes
    tmpl_count, blocks, batch_count, stretch_len = out_ref.shape
    groups = template_rows // tmpl_count
    rows = batch_count * tmpl_count
    taps_count = comp_count * span_len
    body = blocks * tiles
    held = body + edge_tiles
    at = halves * batch_count * template_rows
    edges = chosen_source(got_ref[:, at:].astype(jnp.float32), lax.axis_index("far") + 1)
    def station_samples(half):
        samples = []
        for comp in range(comp_count):
            at = template_rows + comp * tiles
            parts = [seen_ref[half * blocks + block, at : at + tiles].astype(jnp.float32) for block in range(blocks)]
            at = (half * comp_count + comp) * edge_tiles
            samples.append(parts + [edges[at : at + edge_tiles]])
        return samples

    def build_hankel(all_samples):
        for half in range(halves):
            hankel_ref[half, comp_count * STEP :, :] = jnp.zeros((LANES - comp_count * STEP, held * LANES), jnp.bfloat16)
        row = lax.broadcasted_iota(jnp.int32, (8, LANES), 0)
        lane = lax.broadcasted_iota(jnp.int32, (8, LANES), 1)
        for lag in range(0, STEP, 8):
            source = lane + row + lag
            for half in range(halves):
                for comp in range(comp_count):
                    at, later = comp * STEP + lag, 0.0
                    for tile in range(held - 1, -1, -1):
                        block, within = (tile // tiles, tile % tiles) if tile < body else (blocks, tile - body)
                        base = all_samples[half][comp][block][within : within + 1]
                        turned = turn(jnp.broadcast_to(base, (8, LANES)), source)
                        value = jnp.where(source < LANES, turned, later).astype(jnp.bfloat16)
                        hankel_ref[half, at : at + 8, tile * LANES : (tile + 1) * LANES] = value
                        later = turned

    height = up_to(held + 1, 8)

    def inverse_energy(all_samples):
        rows = []
        for samples in all_samples:
            squares = None
            for comp in range(comp_count):
                series = jnp.concatenate(samples[comp] + [jnp.zeros((height - held, LANES), jnp.float32)], axis=0)
                squares = series * series if squares is None else squares + series * series
            rows.append(squares)
        first = jnp.concatenate(rows, axis=0)
        total_rows = first.shape[0]
        reach = up_to(LANES + span_len, LANES) // LANES
        sides = [first] + [pltpu.roll(first, total_rows - side, 0) for side in range(1, reach)]
        wide = jnp.concatenate(sides, axis=1)

        def ahead(value, amount):
            return pltpu.roll(value, reach * LANES - amount, 1)[:, : value.shape[1]] if amount else value

        sums, width = {1: wide}, 1
        while 2 * width <= min(span_len, LANES // 2):
            sums[2 * width] = sums[width] + ahead(sums[width], width)
            width *= 2
        total, at = None, 0
        for width in sorted(sums, reverse=True):
            while span_len - at >= width:
                piece = ahead(sums[width], at)[:, :LANES]
                total = piece if total is None else total + piece
                at += width
        scale = 1.0 / jnp.sqrt(total / taps_count + eps)
        return [scale[i * height : (i + 1) * height] for i in range(len(all_samples))]

    for b in range(batch_count):
        at = b * halves * template_rows
        got = got_ref[:, at : at + halves * template_rows].astype(jnp.float32)
        source = owners_ref[b, 0:1, 0:1] // blocks
        tap_ref[at : at + halves * template_rows, :] = chosen_source(got, source[None])
    step = lax.broadcasted_iota(jnp.int32, (rows, LANES), 1)
    slot = lax.broadcasted_iota(jnp.int32, (rows, LANES), 0)
    lefts, gains, sources = [], [], []
    all_samples = [station_samples(half) for half in range(halves)]
    scales = inverse_energy(all_samples)
    build_hankel(all_samples)
    for half in range(halves):
        taps = []
        for group in range(groups):
            for b in range(batch_count):
                start = (b * halves + half) * template_rows + group
                taps.append(tap_ref[pl.ds(start, tmpl_count, stride=groups), :])
        left = jnp.concatenate(taps, axis=0)
        power = sum(left[g * rows : (g + 1) * rows] * left[g * rows : (g + 1) * rows] for g in range(groups))
        power = jnp.sum(power, axis=1, keepdims=True) / taps_count
        gains.append(1.0 / (taps_count * jnp.sqrt(power + eps)))
        lefts.append(left.astype(jnp.bfloat16))
        at = template_rows + comp_count * tiles
        delays = jnp.broadcast_to(seen_ref[half * blocks, at : at + 1].astype(jnp.float32), (rows, LANES))
        lags = jnp.sum(jnp.where(step == slot, delays, 0.0), axis=1, keepdims=True)
        sources.append(step + lags.astype(jnp.int32))
    for half in range(halves):
        prods = jnp.dot(lefts[half], hankel_ref[half], preferred_element_type=jnp.float32)
        after = None
        for tile in range(held - 1, -1, -1):
            at = tile * LANES
            turned = [prods[:rows, at : at + LANES]]
            for group in range(1, groups):
                part = prods[group * rows : (group + 1) * rows, at : at + LANES]
                turned.append(pltpu.roll(part, LANES - group * STEP, 1))
            if tile <= body:
                prod = turned[0]
                for group in range(1, groups):
                    prod += jnp.where(step < LANES - group * STEP, turned[group], after[group])
                score_ref[half, :, at : at + LANES] = prod * gains[half] * scales[half][tile : tile + 1]
            after = turned
    totals = [None] * body
    for half in range(halves):
        later = None
        for tile in range(body, -1, -1):
            scores = turn(score_ref[half, :, tile * LANES : (tile + 1) * LANES], sources[half])
            if tile < body:
                shifted = jnp.where(sources[half] < LANES, scores, later)
                totals[tile] = shifted if half == 0 else totals[tile] + shifted
            later = scores
    for tile in range(body):
        block, within = tile // tiles, tile % tiles
        for b in range(batch_count):
            part = totals[tile][b * tmpl_count : (b + 1) * tmpl_count]
            out_ref[:, block, b, within * LANES : (within + 1) * LANES] = part


def stack(owners, seen, got, span_len, sizes, out_shape):
    template_rows, comp_count, tiles, edge_tiles, halves = sizes
    held = out_shape[1] * tiles + edge_tiles
    return pl.pallas_call(
        lambda *refs: stack_kernel(span_len, sizes, *refs),
        out_shape=jax.ShapeDtypeStruct(out_shape, jnp.float32),
        in_specs=[VMEM] * 3,
        out_specs=VMEM,
        scratch_shapes=[
            pltpu.VMEM((halves, LANES, held * LANES), jnp.bfloat16),
            pltpu.VMEM((owners.shape[0] * halves * template_rows, LANES), jnp.float32),
            pltpu.VMEM((halves, out_shape[0] * out_shape[2], held * LANES), jnp.float32),
        ],
        compiler_params=LIMIT,
        name="stack",
        cost_estimate=pl.CostEstimate(flops=60_000_000, bytes_accessed=2_000_000, transcendentals=4096),
    )(owners, seen, got)


def shards(data, bank, owners, moveouts):
    local_sta, comp_count, stretch_len = data.shape
    span_len = bank.shape[-1]
    tmpl_count = bank.shape[1]
    batch_count = owners.shape[0]
    far, near, across, halves = (lax.axis_size(axis) for axis in ("far", "near", "across", "half"))
    tiles = stretch_len // LANES
    share = tmpl_count // halves
    sizes = (share * (up_to(span_len, STEP) // STEP), comp_count, tiles, 2, halves)

    def exchange(value, axis):
        return lax.all_to_all(value, axis, 0, 0, tiled=True)

    lags = moveouts.reshape(batch_count * tmpl_count, local_sta)
    slot, owned = pack(jnp.transpose(bank[0], (0, 2, 1, 3)), jnp.transpose(data, (1, 0, 2)), owners[None], lags, halves)
    seen = exchange(slot, ("half", "near"))
    got = exchange(forward(owned, seen, far, sizes), "far")
    scores = stack(owned, seen, got, span_len, sizes, (share, near, batch_count, stretch_len))
    pieces = exchange(scores.reshape(near * across, batch_count, stretch_len), ("across", "near"))
    return jnp.sum(pieces, axis=0)[:, None, :]


def solution(mesh):
    blocks, groups = mesh.devices.shape
    near, halves = 8, 2
    shape = (blocks // near, near, groups // halves, halves)
    split = Mesh(mesh.devices.reshape(shape), ("far", "near", "across", "half"))
    time, sta = ("far", "near"), ("across", "half")
    placed = (P(sta, None, time), P(time, None, sta, None, None), P(), P(None, None, sta))
    return jax.shard_map(
        shards, mesh=split, in_specs=placed, out_specs=P(None, sta, time), check_vma=False
    )
```
